256 devices in a mesh: pipe: 2 (over core), slab: 8 (over x, z_hi), dp: 16 (over z_lo, y).
Axes of the slice: x: 4, y: 4, z: 8 (z_hi: 2, z_lo: 4; z = z_hi * 4 + z_lo), core: 2. Of those that a mesh axis runs over, the one named last changes fastest.
Arguments:
- saved_inputs: bfloat16 [2, 2, 16, 2, 16, 16, 512], P('pipe', None, 'dp', None, 'slab'), may hold values from -12 to 12
- loss_cotangent: bfloat16 [2, 16, 2, 16, 16, 512], P(None, 'dp', None, 'slab'), may hold values from -3 to 3
- upstream: bfloat16 [16, 2, 16, 16, 512], P('dp', None, 'slab'), may hold values from -3 to 3
- conv_weight: bfloat16 [2, 512, 13824], P('pipe', 'dp'), may hold values from -0.0546875 to 0.0546875
- adagn_table: bfloat16 [2, 1000, 1024], P('pipe'), may hold values from -3 to 3
- timesteps: int32 [3, 16], P(None, 'dp'), may hold values from 0 to 999
- frame_counts: int32 [3, 16], P(None, 'dp'), may hold values from 1 to 2
Outputs:
- input_grads: bfloat16 [2, 2, 16, 2, 16, 16, 512], P('pipe', None, 'dp', None, 'slab')
- weight_grad: float32 [2, 512, 13824], P('pipe', 'dp')
- embed_grad: float32 [2, 2, 16, 1024], P('pipe', None, 'dp')
The draws below stay inside these ranges and needn't reach their ends.
All inputs are finite; a program needn't handle non-finite values.
Results may differ from the reference program's by a relative error of at most 0.015.
Values may be sent and summed in bfloat16 or wider, within the bound.
A program may use at most 128 MiB of HBM per device.

```python
import math
import jax
import jax.numpy as jnp
from jax import lax

CH = 512
GROUPS = 32
TABLE = 1000
FR = 2
HS = 2
WID = 16
TICKS = 2
BATCH = 16
HEIGHT = 16
MICRO = 3


def draw_saved_inputs(key, part):
    shape = (2, TICKS, BATCH, FR, HEIGHT, WID, CH)
    key_noise, key_mean, key_chan, key_cell = jax.random.split(key, 4)
    chan_scale = jnp.exp(jax.random.uniform(key_chan, (2, TICKS, BATCH, 1, 1, 1, CH), jnp.float32, math.log(0.3), math.log(3.0)))
    mean_part = 0.8 * jnp.clip(jax.random.normal(key_mean, (2, TICKS, BATCH, 1, 1, 1, CH), jnp.float32), -3.0, 3.0)
    noise = jnp.clip(jax.random.normal(key_noise, shape, jnp.float32), -4.0, 4.0)
    cell_scale = jnp.exp(jax.random.uniform(key_cell, (2, TICKS, BATCH, FR, HEIGHT, WID, 1), jnp.float32, math.log(0.3), math.log(3.0)))
    return (0.125 * (mean_part + noise) * chan_scale * cell_scale).astype(jnp.bfloat16)


def place_ends(array, rng, smallest, high):
    index_at = [jax.random.randint(jax.random.fold_in(rng, axis), (), 0, length) for axis, length in enumerate(array.shape)]
    main_axis = array.shape.index(max(array.shape))
    beside = index_at[:main_axis] + [(index_at[main_axis] + 1) % array.shape[main_axis]] + index_at[main_axis + 1:]
    return array.at[tuple(index_at)].set(smallest).at[tuple(beside)].set(high)


def spiked(array, own_key, source, target, parts, factor):
    owner, partner = [(jnp.arange(array.shape[dim]) // (array.shape[dim] // parts)).reshape([-1 if axis == dim else 1 for axis in range(array.ndim)]) for dim in (source, target)]
    chosen = jax.random.permutation(own_key, parts)[partner]
    strong = (owner == chosen) | (owner == (partner + parts // 2) % parts)
    return jnp.where(strong, factor * array, array)


def steps_of(rng, shape, shards, least, top_value):
    level = 1.0
    for axis_at, blocks in shards:
        draws = jax.random.uniform(jax.random.fold_in(jax.random.fold_in(rng, 6), axis_at), (blocks,), jnp.float32, least / len(shards), top_value / len(shards))
        level = level * jnp.repeat(jnp.exp(draws), shape[axis_at] // blocks).reshape((-1,) + (1,) * (len(shape) - 1 - axis_at))
    return level


def normal_values(stream_key, dims, spread, reach, pieces=(), held_as=jnp.bfloat16):
    values = jax.random.normal(stream_key, dims, jnp.float32) * spread
    if len(pieces) > 0:
        values = steps_of(stream_key, dims, pieces, -0.22, 0.18) * values
    return jnp.clip(values, min=-reach, max=reach).astype(held_as)


def noise_with(own_key, extent, width, most, cuts, heavy, kind=jnp.bfloat16):
    array = width * jax.random.normal(own_key, extent, jnp.float32)
    if cuts:
        array = array * steps_of(own_key, extent, cuts, -0.22, 0.18)
    return jnp.clip(spiked(array, jax.random.fold_in(own_key, 3), *heavy), -most, most).astype(kind)


def setup_inputs(seed: int = 0) -> dict:
    key_of = jax.random.split(jax.random.key(seed), 8)
    saved_inputs = draw_saved_inputs(jax.random.fold_in(key_of[7], 71), 0)
    loss_cotangent = noise_with(key_of[1], (TICKS, BATCH, FR, HEIGHT, WID, CH), 0.5, 3.0, ((1, 16), (3, 8)), (1, 5, 16, 2.0))
    upstream = noise_with(key_of[2], (BATCH, FR, HEIGHT, WID, CH), 0.5, 3.0, ((0, 16), (2, 8)), (0, 4, 16, 2.0))
    conv_weight = normal_values(key_of[3], (2, CH, 27 * CH), (27 * CH) ** -0.5, 0.0546875, ((0, 2), (1, 16)))
    adagn_table = normal_values(key_of[4], (2, TABLE, 2 * CH), 0.5, 3.0, ((0, 2),))
    timesteps = place_ends(jax.random.randint(key_of[5], (MICRO, BATCH), 0, TABLE), jax.random.fold_in(key_of[5], 1), 0, TABLE - 1).astype(jnp.int32)
    frame_counts = place_ends(jax.random.randint(key_of[6], (MICRO, BATCH), 1, FR + 1), jax.random.fold_in(key_of[6], 1), 1, FR).astype(jnp.int32)
    return {"saved_inputs": saved_inputs, "loss_cotangent": loss_cotangent, "upstream": upstream, "conv_weight": conv_weight, "adagn_table": adagn_table, "timesteps": timesteps, "frame_counts": frame_counts}


EPS = 1e-05

def silu_grad(preact):
    sigma = jax.nn.sigmoid(preact)
    return sigma * (1.0 + preact * (1.0 - sigma))

def pad_cells(values):
    return jnp.pad(values, ((0, 0), (1, 1), (1, 1), (1, 1), (0, 0)))

def grouped_sum(values):
    per_group = CH // GROUPS
    return lax.optimization_barrier(jnp.sum(values.reshape(values.shape[0], -1, GROUPS, per_group), axis=(1, 3)))

def spread_groups(per_sample):
    return jnp.repeat(per_sample, CH // GROUPS, axis=1)[:, None, None, None, :]

def block_backward(inputs, cotangent, weight, step_table, steps_now, counts_now):
    onehot = (steps_now[:, None] == jnp.arange(TABLE, dtype=jnp.int32)[None, :]).astype(jnp.float32)
    embedded = jnp.dot(onehot, step_table.astype(jnp.float32), preferred_element_type=jnp.float32, precision=lax.Precision.HIGHEST)
    gains = (1.0 + embedded[:, :CH])[:, None, None, None, :]
    biases = embedded[:, CH:][:, None, None, None, :]
    frame_mask = (jnp.arange(FR, dtype=jnp.int32)[None, :] < counts_now[:, None]).astype(jnp.float32)
    mask_cells = frame_mask[:, :, None, None, None]
    valid = (counts_now.astype(jnp.float32) * float(HEIGHT * WID * (CH // GROUPS)))[:, None]
    values = inputs.astype(jnp.float32)
    mean_g = grouped_sum(values * mask_cells) / valid
    var_g = grouped_sum(values * mask_cells * values) / valid - mean_g * mean_g
    rstd_g = lax.rsqrt(var_g + EPS)
    normed = (values - spread_groups(mean_g)) * spread_groups(rstd_g)
    preact = normed * gains + biases
    hidden = (jax.nn.silu(preact) * mask_cells).astype(jnp.bfloat16)
    cot_pad = pad_cells(cotangent.astype(jnp.float32))
    weight3 = weight.astype(jnp.float32).reshape(CH, 27, CH)
    upward = jnp.zeros(values.shape, jnp.float32)
    for depth_at in range(3):
        for vertical in range(3):
            for across in range(3):
                tap_index = 9 * depth_at + 3 * vertical + across
                shifted = cot_pad[:, 2 - depth_at:2 - depth_at + FR, 2 - vertical:2 - vertical + HEIGHT, 2 - across:2 - across + WID, :]
                upward = upward + jnp.einsum('bfhwo,oi->bfhwi', shifted, weight3[:, tap_index, :])
    pre_grad = upward * silu_grad(preact) * mask_cells
    dnormed = pre_grad * gains
    sum_a = grouped_sum(dnormed) / valid
    sum_b = grouped_sum(dnormed * normed) / valid
    branch = spread_groups(rstd_g) * (dnormed - spread_groups(sum_a) - normed * spread_groups(sum_b)) * mask_cells
    result = (cotangent.astype(jnp.float32) + branch).astype(jnp.bfloat16)
    norm_embed = 1.0 / math.sqrt(FR * HEIGHT * WID)
    embed = jnp.concatenate([lax.optimization_barrier(jnp.sum(pre_grad * normed, axis=(1, 2, 3))), lax.optimization_barrier(jnp.sum(pre_grad, axis=(1, 2, 3)))], axis=1) * norm_embed
    return (result, embed, hidden)

def weight_grads(hidden_list, cot_list):
    hidden_pad = jnp.pad(jnp.stack(hidden_list), ((0, 0), (0, 0), (1, 1), (1, 1), (1, 1), (0, 0)))
    cot_all = jnp.stack(cot_list)
    scale_norm = 1.0 / math.sqrt(TICKS * BATCH * FR * HEIGHT * WID)
    zero = jnp.zeros((), jnp.int32)

    def pair_term(running, pair_index):
        slab_at = (pair_index // BATCH).astype(jnp.int32)
        sample = (pair_index % BATCH).astype(jnp.int32)
        row_start = (slab_at * HS).astype(jnp.int32)
        cot_part = lax.dynamic_slice(cot_all, (zero, sample, zero, row_start, zero, zero), (TICKS, 1, FR, HS, WID, CH)).astype(jnp.float32)
        hid_part = lax.dynamic_slice(hidden_pad, (zero, sample, zero, row_start, zero, zero), (TICKS, 1, FR + 2, HS + 2, WID + 2, CH)).astype(jnp.float32)
        columns = []
        for depth_at in range(3):
            for vertical in range(3):
                for across in range(3):
                    shifted = hid_part[:, :, depth_at:depth_at + FR, vertical:vertical + HS, across:across + WID, :]
                    columns.append(jnp.einsum('kbfhwo,kbfhwi->oi', cot_part, shifted))
        grad_term = jnp.stack(columns, axis=1).reshape(CH, 27 * CH) * scale_norm
        rounded = lax.optimization_barrier(grad_term.astype(jnp.bfloat16))
        return (running + rounded.astype(jnp.float32), None)
    running, unused = lax.scan(pair_term, jnp.zeros((CH, 27 * CH), jnp.float32), jnp.arange(HEIGHT // HS * BATCH, dtype=jnp.int32))
    return running

def reference(saved_inputs, loss_cotangent, upstream, conv_weight, adagn_table, timesteps, frame_counts):
    later_dx, later_embed, later_hidden, later_cot = ([], [], [], [])
    for tick_index in range(TICKS):
        cotangent = loss_cotangent[tick_index]
        result, embed, hidden = block_backward(saved_inputs[1, tick_index], cotangent, conv_weight[1], adagn_table[1], timesteps[tick_index + 1], frame_counts[tick_index + 1])
        later_dx.append(result)
        later_embed.append(embed)
        later_hidden.append(hidden)
        later_cot.append(cotangent)
    early_dx, early_embed, early_hidden, early_cot = ([], [], [], [])
    for tick_index in range(TICKS):
        cotangent = upstream if tick_index == 0 else later_dx[tick_index - 1]
        result, embed, hidden = block_backward(saved_inputs[0, tick_index], cotangent, conv_weight[0], adagn_table[0], timesteps[tick_index], frame_counts[tick_index])
        early_dx.append(result)
        early_embed.append(embed)
        early_hidden.append(hidden)
        early_cot.append(cotangent)
    input_grads = jnp.stack([jnp.stack(early_dx), jnp.stack(later_dx)])
    weight_grad = jnp.stack([weight_grads(early_hidden, early_cot), weight_grads(later_hidden, later_cot)])
    embed_grad = jnp.stack([jnp.stack(early_embed), jnp.stack(later_embed)])
    return (input_grads, weight_grad, embed_grad)
```

```python
import math

import jax
import jax.numpy as jnp
from jax import lax
from jax.sharding import PartitionSpec as P

GROUPS = 32


EPS = 1e-05


def silu_grad(preact):
    sigma = jax.nn.sigmoid(preact)
    return sigma * (1.0 + preact * (1.0 - sigma))


def chunk_group_sums(values, groups_here):
    summed = jnp.sum(values.reshape(-1, values.shape[-1]), axis=0)
    return jnp.sum(summed.reshape(groups_here, -1), axis=1)


def tap_stack(padded, frames, rows, cells_wide):
    slices = []
    for depth_at in range(3):
        for vertical in range(3):
            for across in range(3):
                slices.append(
                    padded[
                        ...,
                        depth_at : depth_at + frames,
                        vertical : vertical + rows,
                        across : across + cells_wide,
                        :,
                    ]
                )
    return jnp.stack(slices, 0)


def local(
    saved_inputs, loss_cotangent, upstream, conv_weight, adagn_table, timesteps, frame_counts
):
    section_index = lax.axis_index("pipe")
    slab_index = lax.axis_index("slab")
    slab_count = lax.axis_size("slab")
    replicas = lax.axis_size("dp")
    inputs = saved_inputs[0, :, 0]
    tick_count, frames, slab_rows, cells_wide, channels = inputs.shape
    height_total = slab_rows * slab_count
    chunk = channels // slab_count
    per_group = channels // GROUPS
    groups_here = chunk // per_group
    step_table = adagn_table[0]
    taps = 27
    weight_local = conv_weight[0].reshape(-1, taps, channels)
    steps_now = lax.dynamic_slice_in_dim(timesteps[:, 0], section_index, tick_count)
    counts_now = lax.dynamic_slice_in_dim(frame_counts[:, 0], section_index, tick_count)
    chunk_start = slab_index * chunk

    weight_cols = lax.dynamic_slice_in_dim(weight_local, chunk_start, chunk, axis=2)
    weight_chunk = lax.all_gather(weight_cols, "dp", axis=0, tiled=True)
    kernel = weight_chunk.reshape(channels, 3, 3, 3, chunk)[:, ::-1, ::-1, ::-1, :]
    kernel = jnp.transpose(kernel, (1, 2, 3, 0, 4))

    inputs_chunk = lax.all_to_all(inputs, "slab", 4, 2, tiled=True)

    weight_norm = 1.0 / math.sqrt(tick_count * replicas * frames * height_total * cells_wide)
    embed_norm = 1.0 / math.sqrt(frames * height_total * cells_wide)

    def full_rows(rows_value):
        return lax.all_gather(rows_value, "slab", axis=1, tiled=True)

    cot_first = jnp.where(section_index == 1, loss_cotangent[0, 0], upstream[0])
    cot_full_first = full_rows(cot_first)
    cot_full_later = full_rows(loss_cotangent[1, 0])

    dx_list = []
    embed_list = []
    hidden_list = []
    cot_list = []
    cot_full = cot_full_first
    for tick_index in range(tick_count):
        steps = steps_now[tick_index]
        count = counts_now[tick_index]
        embedded = lax.dynamic_index_in_dim(step_table, steps, keepdims=False).astype(
            jnp.float32
        )
        gain = 1.0 + lax.dynamic_slice_in_dim(embedded, chunk_start, chunk)
        bias = lax.dynamic_slice_in_dim(embedded, channels + chunk_start, chunk)
        mask = (jnp.arange(frames, dtype=jnp.int32) < count).astype(jnp.float32)
        mask_cells = mask[:, None, None, None]
        valid = count.astype(jnp.float32) * float(height_total * cells_wide * per_group)

        values = inputs_chunk[tick_index].astype(jnp.float32)
        masked = values * mask_cells
        mean_g = chunk_group_sums(masked, groups_here) / valid
        var_g = chunk_group_sums(masked * values, groups_here) / valid - mean_g * mean_g
        rstd_g = lax.rsqrt(var_g + EPS)
        mean_c = jnp.repeat(mean_g, per_group)
        rstd_c = jnp.repeat(rstd_g, per_group)
        normed = (values - mean_c) * rstd_c
        preact = normed * gain + bias
        hidden = (jax.nn.silu(preact) * mask_cells).astype(jnp.bfloat16)
        hidden_list.append(hidden)

        upward = lax.conv_general_dilated(
            cot_full[None],
            kernel,
            window_strides=(1, 1, 1),
            padding=((1, 1), (1, 1), (1, 1)),
            dimension_numbers=("NDHWC", "DHWIO", "NDHWC"),
            preferred_element_type=jnp.float32,
        )[0]
        pre_grad = upward * silu_grad(preact) * mask_cells
        dnormed = pre_grad * gain
        sum_a = chunk_group_sums(dnormed, groups_here) / valid
        sum_b = chunk_group_sums(dnormed * normed, groups_here) / valid
        scale_part = jnp.sum(pre_grad * normed, axis=(0, 1, 2))
        shift_part = jnp.sum(pre_grad, axis=(0, 1, 2))
        branch = (
            rstd_c
            * (dnormed - jnp.repeat(sum_a, per_group) - normed * jnp.repeat(sum_b, per_group))
            * mask_cells
        )
        cot_chunk = lax.dynamic_slice_in_dim(cot_full, chunk_start, chunk, axis=3)
        result = (cot_chunk.astype(jnp.float32) + branch).astype(jnp.bfloat16)
        result_full = lax.all_gather(result, "slab", axis=3, tiled=True)
        dx_list.append(
            lax.dynamic_slice_in_dim(result_full, slab_index * slab_rows, slab_rows, axis=1)
        )
        embed_list.append(jnp.stack([scale_part, shift_part]))
        cot_list.append(cot_full)
        if tick_index + 1 < tick_count:
            received = lax.ppermute(result_full, "pipe", [(1, 0)])
            cot_full = jnp.where(section_index == 1, cot_full_later, received)

    embed_all = lax.all_gather(jnp.stack(embed_list), "slab", axis=2, tiled=True)
    embed_grad = embed_all.reshape(tick_count, 2 * channels) * embed_norm

    cot_all = jnp.stack(cot_list)
    hidden_all = jnp.pad(
        jnp.stack(hidden_list), ((0, 0), (1, 1), (1, 1), (1, 1), (0, 0))
    )
    hidden_taps = tap_stack(hidden_all, frames, height_total, cells_wide)
    grad_term = jnp.einsum(
        "kfrwo,tkfrwi->oti", cot_all, hidden_taps, preferred_element_type=jnp.float32
    )
    grad_shard = lax.psum_scatter(
        (grad_term * weight_norm).astype(jnp.bfloat16),
        "dp",
        scatter_dimension=0,
        tiled=True,
    ).astype(jnp.float32)
    weight_grad = lax.all_gather(grad_shard, "slab", axis=2, tiled=True)
    weight_grad = weight_grad.reshape(weight_grad.shape[0], taps * channels)
    input_grads = jnp.stack(dx_list)[None, :, None]
    return (input_grads, weight_grad[None], embed_grad[None, :, None])


def solution(mesh):
    placed = (
        P("pipe", None, "dp", None, "slab", None, None),
        P(None, "dp", None, "slab", None, None),
        P("dp", None, "slab", None, None),
        P("pipe", "dp", None),
        P("pipe", None, None),
        P(None, "dp"),
        P(None, "dp"),
    )
    return jax.shard_map(
        local,
        mesh=mesh,
        in_specs=placed,
        out_specs=(
            P("pipe", None, "dp", None, "slab", None, None),
            P("pipe", "dp", None),
            P("pipe", None, "dp", None),
        ),
        check_vma=False,
    )
```

```python
import math

import jax
import jax.numpy as jnp
from jax import lax
from jax.sharding import PartitionSpec as P

GROUPS = 32


EPS = 1e-05


def silu_grad(preact):
    sigma = jax.nn.sigmoid(preact)
    return sigma * (1.0 + preact * (1.0 - sigma))


def chunk_group_sums(values, groups_here):
    summed = jnp.sum(values.reshape(-1, values.shape[-1]), axis=0)
    return jnp.sum(summed.reshape(groups_here, -1), axis=1)


def shifted_copies(value, axis):
    devices = lax.axis_size(axis)
    pieces = [value]
    for distance in range(1, devices):
        route = [(i, (i + distance) % devices) for i in range(devices)]
        pieces.append(lax.ppermute(value, axis, route))
    return pieces


def gather_stack(value, axis):
    devices = lax.axis_size(axis)
    here = lax.axis_index(axis)
    stacked = jnp.stack(shifted_copies(value, axis))
    order = (here - jnp.arange(devices, dtype=jnp.int32)) % devices
    return jnp.take(stacked, order, axis=0)


def exchange_blocks(blocks, axis):
    devices = lax.axis_size(axis)
    here = lax.axis_index(axis)
    pieces = [lax.dynamic_index_in_dim(blocks, here, keepdims=False)]
    for distance in range(1, devices):
        route = [(i, (i + distance) % devices) for i in range(devices)]
        target = (here + distance) % devices
        pieces.append(
            lax.ppermute(lax.dynamic_index_in_dim(blocks, target, keepdims=False), axis, route)
        )
    stacked = jnp.stack(pieces)
    order = (here - jnp.arange(devices, dtype=jnp.int32)) % devices
    return jnp.take(stacked, order, axis=0)


def scatter_sum(blocks, axis):
    devices = lax.axis_size(axis)
    here = lax.axis_index(axis)
    total = lax.dynamic_index_in_dim(blocks, here, keepdims=False).astype(jnp.float32)
    for distance in range(1, devices):
        route = [(i, (i + distance) % devices) for i in range(devices)]
        target = (here + distance) % devices
        sent = lax.dynamic_index_in_dim(blocks, target, keepdims=False)
        total = total + lax.ppermute(sent, axis, route).astype(jnp.float32)
    return total


def tap_stack(padded, frames, rows, cells_wide):
    slices = []
    for depth_at in range(3):
        for vertical in range(3):
            for across in range(3):
                slices.append(
                    padded[
                        ...,
                        depth_at : depth_at + frames,
                        vertical : vertical + rows,
                        across : across + cells_wide,
                        :,
                    ]
                )
    return jnp.stack(slices, 0)


def local(
    saved_inputs, loss_cotangent, upstream, conv_weight, adagn_table, timesteps, frame_counts
):
    section_index = lax.axis_index("pipe")
    slab_index = lax.axis_index("slab")
    slab_count = lax.axis_size("slab")
    replicas = lax.axis_size("dp")
    inputs = saved_inputs[0, :, 0]
    tick_count, frames, slab_rows, cells_wide, channels = inputs.shape
    height_total = slab_rows * slab_count
    chunk = channels // slab_count
    per_group = channels // GROUPS
    groups_here = chunk // per_group
    step_table = adagn_table[0]
    taps = 27
    weight_local = conv_weight[0].reshape(-1, taps, channels)
    steps_now = lax.dynamic_slice_in_dim(timesteps[:, 0], section_index, tick_count)
    counts_now = lax.dynamic_slice_in_dim(frame_counts[:, 0], section_index, tick_count)
    chunk_start = slab_index * chunk

    weight_cols = lax.dynamic_slice_in_dim(weight_local, chunk_start, chunk, axis=2)
    weight_chunk = gather_stack(weight_cols, "dp")
    kernel = weight_chunk.reshape(channels, 3, 3, 3, chunk)[:, ::-1, ::-1, ::-1, :]
    kernel = jnp.transpose(kernel, (1, 2, 3, 0, 4))

    outgoing = inputs.reshape(tick_count, frames, slab_rows, cells_wide, slab_count, chunk)
    outgoing = jnp.transpose(outgoing, (4, 0, 1, 2, 3, 5))
    incoming = exchange_blocks(outgoing, "slab")
    inputs_chunk = jnp.transpose(incoming, (1, 2, 0, 3, 4, 5)).reshape(
        tick_count, frames, height_total, cells_wide, chunk
    )

    weight_norm = 1.0 / math.sqrt(tick_count * replicas * frames * height_total * cells_wide)
    embed_norm = 1.0 / math.sqrt(frames * height_total * cells_wide)

    cot_first = jnp.where(section_index == 1, loss_cotangent[0, 0], upstream[0])
    cot_both = gather_stack(jnp.stack([cot_first, loss_cotangent[1, 0]]), "slab")
    cot_both = jnp.transpose(cot_both, (1, 2, 0, 3, 4, 5)).reshape(
        tick_count, frames, height_total, cells_wide, channels
    )
    cot_full_first = cot_both[0]
    cot_full_later = cot_both[1]

    dx_list = []
    embed_list = []
    hidden_list = []
    cot_list = []
    cot_full = cot_full_first
    for tick_index in range(tick_count):
        steps = steps_now[tick_index]
        count = counts_now[tick_index]
        embedded = lax.dynamic_index_in_dim(step_table, steps, keepdims=False).astype(
            jnp.float32
        )
        gain = 1.0 + lax.dynamic_slice_in_dim(embedded, chunk_start, chunk)
        bias = lax.dynamic_slice_in_dim(embedded, channels + chunk_start, chunk)
        mask = (jnp.arange(frames, dtype=jnp.int32) < count).astype(jnp.float32)
        mask_cells = mask[:, None, None, None]
        valid = count.astype(jnp.float32) * float(height_total * cells_wide * per_group)

        values = inputs_chunk[tick_index].astype(jnp.float32)
        masked = values * mask_cells
        mean_g = chunk_group_sums(masked, groups_here) / valid
        var_g = chunk_group_sums(masked * values, groups_here) / valid - mean_g * mean_g
        rstd_g = lax.rsqrt(var_g + EPS)
        mean_c = jnp.repeat(mean_g, per_group)
        rstd_c = jnp.repeat(rstd_g, per_group)
        normed = (values - mean_c) * rstd_c
        preact = normed * gain + bias
        hidden = (jax.nn.silu(preact) * mask_cells).astype(jnp.bfloat16)
        hidden_list.append(hidden)

        upward = lax.conv_general_dilated(
            cot_full[None],
            kernel,
            window_strides=(1, 1, 1),
            padding=((1, 1), (1, 1), (1, 1)),
            dimension_numbers=("NDHWC", "DHWIO", "NDHWC"),
            preferred_element_type=jnp.float32,
        )[0]
        pre_grad = upward * silu_grad(preact) * mask_cells
        dnormed = pre_grad * gain
        sum_a = chunk_group_sums(dnormed, groups_here) / valid
        sum_b = chunk_group_sums(dnormed * normed, groups_here) / valid
        scale_part = jnp.sum(pre_grad * normed, axis=(0, 1, 2))
        shift_part = jnp.sum(pre_grad, axis=(0, 1, 2))
        branch = (
            rstd_c
            * (dnormed - jnp.repeat(sum_a, per_group) - normed * jnp.repeat(sum_b, per_group))
            * mask_cells
        )
        cot_chunk = lax.dynamic_slice_in_dim(cot_full, chunk_start, chunk, axis=3)
        result = (cot_chunk.astype(jnp.float32) + branch).astype(jnp.bfloat16)
        if tick_index + 1 < tick_count:
            result_full = jnp.transpose(gather_stack(result, "slab"), (1, 2, 3, 0, 4)).reshape(
                frames, height_total, cells_wide, channels
            )
            dx_list.append(
                lax.dynamic_slice_in_dim(result_full, slab_index * slab_rows, slab_rows, axis=1)
            )
        else:
            outgoing = jnp.transpose(
                result.reshape(frames, slab_count, slab_rows, cells_wide, chunk), (1, 0, 2, 3, 4)
            )
            incoming = exchange_blocks(outgoing, "slab")
            dx_list.append(
                jnp.transpose(incoming, (1, 2, 3, 0, 4)).reshape(
                    frames, slab_rows, cells_wide, channels
                )
            )
        embed_list.append(jnp.stack([scale_part, shift_part]))
        cot_list.append(cot_full)
        if tick_index + 1 < tick_count:
            received = lax.ppermute(result_full, "pipe", [(1, 0)])
            cot_full = jnp.where(section_index == 1, cot_full_later, received)

    embed_all = jnp.transpose(gather_stack(jnp.stack(embed_list), "slab"), (1, 2, 0, 3))
    embed_grad = embed_all.reshape(tick_count, 2 * channels) * embed_norm

    cot_all = jnp.stack(cot_list)
    hidden_all = jnp.pad(
        jnp.stack(hidden_list), ((0, 0), (1, 1), (1, 1), (1, 1), (0, 0))
    )
    hidden_taps = tap_stack(hidden_all, frames, height_total, cells_wide)
    grad_term = jnp.einsum(
        "kfrwo,tkfrwi->oti", cot_all, hidden_taps, preferred_element_type=jnp.float32
    )
    terms = (grad_term * weight_norm).astype(jnp.bfloat16)
    terms = terms.reshape(replicas, channels // replicas, taps, chunk)
    grad_shard = scatter_sum(terms, "dp")
    weight_grad = jnp.transpose(gather_stack(grad_shard, "slab"), (1, 2, 0, 3))
    weight_grad = weight_grad.reshape(weight_grad.shape[0], taps * channels)
    input_grads = jnp.stack(dx_list)[None, :, None]
    return (input_grads, weight_grad[None], embed_grad[None, :, None])


def solution(mesh):
    placed = (
        P("pipe", None, "dp", None, "slab", None, None),
        P(None, "dp", None, "slab", None, None),
        P("dp", None, "slab", None, None),
        P("pipe", "dp", None),
        P("pipe", None, None),
        P(None, "dp"),
        P(None, "dp"),
    )
    return jax.shard_map(
        local,
        mesh=mesh,
        in_specs=placed,
        out_specs=(
            P("pipe", None, "dp", None, "slab", None, None),
            P("pipe", "dp", None),
            P("pipe", None, "dp", None),
        ),
        check_vma=False,
    )
```

```python
import math

import jax
import jax.numpy as jnp
from jax import lax
from jax.sharding import PartitionSpec as P

GROUPS = 32

DP_INNER = 4
SLAB_INNER = 2


EPS = 1e-05


def silu_grad(preact):
    sigma = jax.nn.sigmoid(preact)
    return sigma * (1.0 + preact * (1.0 - sigma))


def chunk_group_sums(values, groups_here):
    summed = jnp.sum(values.reshape(-1, values.shape[-1]), axis=0)
    return jnp.sum(summed.reshape(groups_here, -1), axis=1)


def shifted_copies(value, axis):
    devices = lax.axis_size(axis)
    pieces = [value]
    for distance in range(1, devices):
        route = [(i, (i + distance) % devices) for i in range(devices)]
        pieces.append(lax.ppermute(value, axis, route))
    return pieces


def gather_stack(value, axis):
    devices = lax.axis_size(axis)
    here = lax.axis_index(axis)
    stacked = jnp.stack(shifted_copies(value, axis))
    order = (here - jnp.arange(devices, dtype=jnp.int32)) % devices
    return jnp.take(stacked, order, axis=0)


def exchange_blocks(blocks, axis):
    devices = lax.axis_size(axis)
    here = lax.axis_index(axis)
    pieces = [lax.dynamic_index_in_dim(blocks, here, keepdims=False)]
    for distance in range(1, devices):
        route = [(i, (i + distance) % devices) for i in range(devices)]
        target = (here + distance) % devices
        pieces.append(
            lax.ppermute(lax.dynamic_index_in_dim(blocks, target, keepdims=False), axis, route)
        )
    stacked = jnp.stack(pieces)
    order = (here - jnp.arange(devices, dtype=jnp.int32)) % devices
    return jnp.take(stacked, order, axis=0)


def scatter_sum(blocks, axis):
    devices = lax.axis_size(axis)
    here = lax.axis_index(axis)
    total = lax.dynamic_index_in_dim(blocks, here, keepdims=False).astype(jnp.float32)
    for distance in range(1, devices):
        route = [(i, (i + distance) % devices) for i in range(devices)]
        target = (here + distance) % devices
        sent = lax.dynamic_index_in_dim(blocks, target, keepdims=False)
        total = total + lax.ppermute(sent, axis, route).astype(jnp.float32)
    return total


def gather_two_level(value, axis, inner):
    devices = lax.axis_size(axis)
    outer = devices // inner
    here = lax.axis_index(axis)
    low = here % inner
    high = here // inner
    pieces = [value]
    for distance in range(1, inner):
        route = [(i, (i // inner) * inner + (i % inner + distance) % inner) for i in range(devices)]
        pieces.append(lax.ppermute(value, axis, route))
    order = (low - jnp.arange(inner, dtype=jnp.int32)) % inner
    level = jnp.take(jnp.stack(pieces), order, axis=0)
    pieces = [level]
    for distance in range(1, outer):
        route = [(i, ((i // inner + distance) % outer) * inner + i % inner) for i in range(devices)]
        pieces.append(lax.ppermute(level, axis, route))
    order = (high - jnp.arange(outer, dtype=jnp.int32)) % outer
    stacked = jnp.take(jnp.stack(pieces), order, axis=0)
    return stacked.reshape((devices,) + value.shape)


def scatter_sum_two_level(blocks, axis, inner):
    devices = lax.axis_size(axis)
    outer = devices // inner
    here = lax.axis_index(axis)
    low = here % inner
    high = here // inner
    grid = blocks.reshape((outer, inner) + blocks.shape[1:])
    partial = lax.dynamic_index_in_dim(grid, high, keepdims=False).astype(jnp.float32)
    for distance in range(1, outer):
        route = [(i, ((i // inner + distance) % outer) * inner + i % inner) for i in range(devices)]
        target = (high + distance) % outer
        sent = lax.dynamic_index_in_dim(grid, target, keepdims=False)
        partial = partial + lax.ppermute(sent, axis, route).astype(jnp.float32)
    total = lax.dynamic_index_in_dim(partial, low, keepdims=False)
    for distance in range(1, inner):
        route = [(i, (i // inner) * inner + (i % inner + distance) % inner) for i in range(devices)]
        target = (low + distance) % inner
        sent = lax.dynamic_index_in_dim(partial, target, keepdims=False)
        total = total + lax.ppermute(sent, axis, route)
    return total


def tap_stack(padded, frames, rows, cells_wide):
    slices = []
    for depth_at in range(3):
        for vertical in range(3):
            for across in range(3):
                slices.append(
                    padded[
                        ...,
                        depth_at : depth_at + frames,
                        vertical : vertical + rows,
                        across : across + cells_wide,
                        :,
                    ]
                )
    return jnp.stack(slices, 0)


def local(
    saved_inputs, loss_cotangent, upstream, conv_weight, adagn_table, timesteps, frame_counts
):
    section_index = lax.axis_index("pipe")
    slab_index = lax.axis_index("slab")
    slab_count = lax.axis_size("slab")
    replicas = lax.axis_size("dp")
    inputs = saved_inputs[0, :, 0]
    tick_count, frames, slab_rows, cells_wide, channels = inputs.shape
    height_total = slab_rows * slab_count
    chunk = channels // slab_count
    per_group = channels // GROUPS
    groups_here = chunk // per_group
    step_table = adagn_table[0]
    taps = 27
    weight_local = conv_weight[0].reshape(-1, taps, channels)
    steps_now = lax.dynamic_slice_in_dim(timesteps[:, 0], section_index, tick_count)
    counts_now = lax.dynamic_slice_in_dim(frame_counts[:, 0], section_index, tick_count)
    chunk_start = slab_index * chunk

    weight_cols = lax.dynamic_slice_in_dim(weight_local, chunk_start, chunk, axis=2)
    weight_chunk = gather_two_level(weight_cols, "dp", DP_INNER)
    kernel = weight_chunk.reshape(channels, 3, 3, 3, chunk)[:, ::-1, ::-1, ::-1, :]
    kernel = jnp.transpose(kernel, (1, 2, 3, 0, 4))


    weight_norm = 1.0 / math.sqrt(tick_count * replicas * frames * height_total * cells_wide)
    embed_norm = 1.0 / math.sqrt(frames * height_total * cells_wide)

    cot_first = jnp.where(section_index == 1, loss_cotangent[0, 0], upstream[0])
    starting = jnp.concatenate([inputs, cot_first[None], loss_cotangent[1, 0][None]])
    gathered = gather_two_level(starting, "slab", SLAB_INNER)
    gathered = jnp.transpose(gathered, (1, 2, 0, 3, 4, 5)).reshape(
        2 * tick_count, frames, height_total, cells_wide, channels
    )
    inputs_chunk = lax.dynamic_slice_in_dim(gathered[:tick_count], chunk_start, chunk, axis=4)
    cot_both = gathered[tick_count:]
    cot_full_first = cot_both[0]
    cot_full_later = cot_both[1]

    dx_list = []
    embed_list = []
    hidden_list = []
    cot_list = []
    cot_full = cot_full_first
    for tick_index in range(tick_count):
        steps = steps_now[tick_index]
        count = counts_now[tick_index]
        embedded = lax.dynamic_index_in_dim(step_table, steps, keepdims=False).astype(
            jnp.float32
        )
        gain = 1.0 + lax.dynamic_slice_in_dim(embedded, chunk_start, chunk)
        bias = lax.dynamic_slice_in_dim(embedded, channels + chunk_start, chunk)
        mask = (jnp.arange(frames, dtype=jnp.int32) < count).astype(jnp.float32)
        mask_cells = mask[:, None, None, None]
        valid = count.astype(jnp.float32) * float(height_total * cells_wide * per_group)

        values = inputs_chunk[tick_index].astype(jnp.float32)
        masked = values * mask_cells
        mean_g = chunk_group_sums(masked, groups_here) / valid
        var_g = chunk_group_sums(masked * values, groups_here) / valid - mean_g * mean_g
        rstd_g = lax.rsqrt(var_g + EPS)
        mean_c = jnp.repeat(mean_g, per_group)
        rstd_c = jnp.repeat(rstd_g, per_group)
        normed = (values - mean_c) * rstd_c
        preact = normed * gain + bias
        hidden = (jax.nn.silu(preact) * mask_cells).astype(jnp.bfloat16)
        hidden_list.append(hidden)

        upward = lax.conv_general_dilated(
            cot_full[None],
            kernel,
            window_strides=(1, 1, 1),
            padding=((1, 1), (1, 1), (1, 1)),
            dimension_numbers=("NDHWC", "DHWIO", "NDHWC"),
            preferred_element_type=jnp.float32,
        )[0]
        pre_grad = upward * silu_grad(preact) * mask_cells
        dnormed = pre_grad * gain
        sum_a = chunk_group_sums(dnormed, groups_here) / valid
        sum_b = chunk_group_sums(dnormed * normed, groups_here) / valid
        scale_part = jnp.sum(pre_grad * normed, axis=(0, 1, 2))
        shift_part = jnp.sum(pre_grad, axis=(0, 1, 2))
        branch = (
            rstd_c
            * (dnormed - jnp.repeat(sum_a, per_group) - normed * jnp.repeat(sum_b, per_group))
            * mask_cells
        )
        cot_chunk = lax.dynamic_slice_in_dim(cot_full, chunk_start, chunk, axis=3)
        result = (cot_chunk.astype(jnp.float32) + branch).astype(jnp.bfloat16)
        embed_list.append(jnp.stack([scale_part, shift_part]))
        if tick_index + 1 < tick_count:
            result_full = jnp.transpose(
                gather_two_level(result, "slab", SLAB_INNER), (1, 2, 3, 0, 4)
            ).reshape(frames, height_total, cells_wide, channels)
        else:
            flat = result.size
            payload = jnp.concatenate(
                [result.astype(jnp.float32).reshape(-1), jnp.stack(embed_list).reshape(-1)]
            )
            collected = gather_two_level(payload, "slab", SLAB_INNER)
            result_full = jnp.transpose(
                collected[:, :flat].reshape((slab_count,) + result.shape), (1, 2, 3, 0, 4)
            ).reshape(frames, height_total, cells_wide, channels).astype(jnp.bfloat16)
            embed_all = jnp.transpose(
                collected[:, flat:].reshape(slab_count, tick_count, 2, chunk), (1, 2, 0, 3)
            )
        dx_list.append(
            lax.dynamic_slice_in_dim(result_full, slab_index * slab_rows, slab_rows, axis=1)
        )
        cot_list.append(cot_full)
        if tick_index + 1 < tick_count:
            received = lax.ppermute(result_full, "pipe", [(1, 0)])
            cot_full = jnp.where(section_index == 1, cot_full_later, received)

    embed_grad = embed_all.reshape(tick_count, 2 * channels) * embed_norm

    cot_all = jnp.stack(cot_list)
    hidden_all = jnp.pad(
        jnp.stack(hidden_list), ((0, 0), (1, 1), (1, 1), (1, 1), (0, 0))
    )
    hidden_taps = tap_stack(hidden_all, frames, height_total, cells_wide)
    grad_term = jnp.einsum(
        "kfrwo,tkfrwi->oti", cot_all, hidden_taps, preferred_element_type=jnp.float32
    )
    terms = (grad_term * weight_norm).astype(jnp.bfloat16)
    terms = terms.reshape(replicas, channels // replicas, taps, chunk)
    grad_shard = scatter_sum_two_level(terms, "dp", DP_INNER)
    weight_grad = jnp.transpose(gather_two_level(grad_shard, "slab", SLAB_INNER), (1, 2, 0, 3))
    weight_grad = weight_grad.reshape(weight_grad.shape[0], taps * channels)
    input_grads = jnp.stack(dx_list)[None, :, None]
    return (input_grads, weight_grad[None], embed_grad[None, :, None])


def solution(mesh):
    placed = (
        P("pipe", None, "dp", None, "slab", None, None),
        P(None, "dp", None, "slab", None, None),
        P("dp", None, "slab", None, None),
        P("pipe", "dp", None),
        P("pipe", None, None),
        P(None, "dp"),
        P(None, "dp"),
    )
    return jax.shard_map(
        local,
        mesh=mesh,
        in_specs=placed,
        out_specs=(
            P("pipe", None, "dp", None, "slab", None, None),
            P("pipe", "dp", None),
            P("pipe", None, "dp", None),
        ),
        check_vma=False,
    )
```

```python
import math

import jax
import jax.numpy as jnp
from jax import lax
from jax.sharding import PartitionSpec as P

GROUPS = 32

DP_INNER = 4
SLAB_INNER = 2


EPS = 1e-05


def silu_grad(preact):
    sigma = jax.nn.sigmoid(preact)
    return sigma * (1.0 + preact * (1.0 - sigma))


def chunk_group_sums(values, groups_here):
    summed = jnp.sum(values.reshape(-1, values.shape[-1]), axis=0)
    return jnp.sum(summed.reshape(groups_here, -1), axis=1)


def shifted_copies(value, axis):
    devices = lax.axis_size(axis)
    pieces = [value]
    for distance in range(1, devices):
        route = [(i, (i + distance) % devices) for i in range(devices)]
        pieces.append(lax.ppermute(value, axis, route))
    return pieces


def gather_stack(value, axis):
    devices = lax.axis_size(axis)
    here = lax.axis_index(axis)
    stacked = jnp.stack(shifted_copies(value, axis))
    order = (here - jnp.arange(devices, dtype=jnp.int32)) % devices
    return jnp.take(stacked, order, axis=0)


def exchange_blocks(blocks, axis):
    devices = lax.axis_size(axis)
    here = lax.axis_index(axis)
    pieces = [lax.dynamic_index_in_dim(blocks, here, keepdims=False)]
    for distance in range(1, devices):
        route = [(i, (i + distance) % devices) for i in range(devices)]
        target = (here + distance) % devices
        pieces.append(
            lax.ppermute(lax.dynamic_index_in_dim(blocks, target, keepdims=False), axis, route)
        )
    stacked = jnp.stack(pieces)
    order = (here - jnp.arange(devices, dtype=jnp.int32)) % devices
    return jnp.take(stacked, order, axis=0)


def scatter_sum(blocks, axis):
    devices = lax.axis_size(axis)
    here = lax.axis_index(axis)
    total = lax.dynamic_index_in_dim(blocks, here, keepdims=False).astype(jnp.float32)
    for distance in range(1, devices):
        route = [(i, (i + distance) % devices) for i in range(devices)]
        target = (here + distance) % devices
        sent = lax.dynamic_index_in_dim(blocks, target, keepdims=False)
        total = total + lax.ppermute(sent, axis, route).astype(jnp.float32)
    return total


def level_routes(devices, inner, along_low, distance):
    outer = devices // inner
    if along_low:
        return [(i, (i // inner) * inner + (i % inner + distance) % inner) for i in range(devices)]
    return [(i, ((i // inner + distance) % outer) * inner + i % inner) for i in range(devices)]


def gather_level(value, axis, inner, along_low):
    devices = lax.axis_size(axis)
    here = lax.axis_index(axis)
    count = inner if along_low else devices // inner
    position = here % inner if along_low else here // inner
    pieces = [value]
    for distance in range(1, count):
        pieces.append(lax.ppermute(value, axis, level_routes(devices, inner, along_low, distance)))
    order = (position - jnp.arange(count, dtype=jnp.int32)) % count
    return jnp.take(jnp.stack(pieces), order, axis=0)


def gather_two_level(value, axis, inner, low_first=True):
    devices = lax.axis_size(axis)
    first = gather_level(value, axis, inner, low_first)
    both = gather_level(first, axis, inner, not low_first)
    if not low_first:
        both = jnp.swapaxes(both, 0, 1)
    return both.reshape((devices,) + value.shape)


def scatter_level(grid, axis, inner, along_low, wire_type):
    devices = lax.axis_size(axis)
    here = lax.axis_index(axis)
    count = inner if along_low else devices // inner
    position = here % inner if along_low else here // inner
    total = lax.dynamic_index_in_dim(grid, position, keepdims=False).astype(jnp.float32)
    for distance in range(1, count):
        target = (position + distance) % count
        sent = lax.dynamic_index_in_dim(grid, target, keepdims=False).astype(wire_type)
        route = level_routes(devices, inner, along_low, distance)
        total = total + lax.ppermute(sent, axis, route).astype(jnp.float32)
    return total


def scatter_sum_two_level(blocks, axis, inner):
    devices = lax.axis_size(axis)
    outer = devices // inner
    grid = blocks.reshape((outer, inner) + blocks.shape[1:])
    partial = scatter_level(jnp.swapaxes(grid, 0, 1), axis, inner, True, blocks.dtype)
    return scatter_level(partial, axis, inner, False, jnp.bfloat16)


def tap_stack(padded, frames, rows, cells_wide):
    slices = []
    for depth_at in range(3):
        for vertical in range(3):
            for across in range(3):
                slices.append(
                    padded[
                        ...,
                        depth_at : depth_at + frames,
                        vertical : vertical + rows,
                        across : across + cells_wide,
                        :,
                    ]
                )
    return jnp.stack(slices, 0)


def local(
    saved_inputs, loss_cotangent, upstream, conv_weight, adagn_table, timesteps, frame_counts
):
    section_index = lax.axis_index("pipe")
    slab_index = lax.axis_index("slab")
    slab_count = lax.axis_size("slab")
    replicas = lax.axis_size("dp")
    inputs = saved_inputs[0, :, 0]
    tick_count, frames, slab_rows, cells_wide, channels = inputs.shape
    height_total = slab_rows * slab_count
    chunk = channels // slab_count
    per_group = channels // GROUPS
    groups_here = chunk // per_group
    step_table = adagn_table[0]
    taps = 27
    weight_local = conv_weight[0].reshape(-1, taps, channels)
    steps_now = lax.dynamic_slice_in_dim(timesteps[:, 0], section_index, tick_count)
    counts_now = lax.dynamic_slice_in_dim(frame_counts[:, 0], section_index, tick_count)
    chunk_start = slab_index * chunk

    weight_cols = lax.dynamic_slice_in_dim(weight_local, chunk_start, chunk, axis=2)
    weight_chunk = gather_two_level(weight_cols, "dp", DP_INNER, low_first=False)
    kernel = weight_chunk.reshape(channels, 3, 3, 3, chunk)[:, ::-1, ::-1, ::-1, :]
    kernel = jnp.transpose(kernel, (1, 2, 3, 0, 4))


    weight_norm = 1.0 / math.sqrt(tick_count * replicas * frames * height_total * cells_wide)
    embed_norm = 1.0 / math.sqrt(frames * height_total * cells_wide)

    cot_first = jnp.where(section_index == 1, loss_cotangent[0, 0], upstream[0])
    starting = jnp.concatenate([inputs, cot_first[None], loss_cotangent[1, 0][None]])
    gathered = gather_two_level(starting, "slab", SLAB_INNER)
    gathered = jnp.transpose(gathered, (1, 2, 0, 3, 4, 5)).reshape(
        2 * tick_count, frames, height_total, cells_wide, channels
    )
    inputs_chunk = lax.dynamic_slice_in_dim(gathered[:tick_count], chunk_start, chunk, axis=4)
    cot_both = gathered[tick_count:]
    cot_full_first = cot_both[0]
    cot_full_later = cot_both[1]

    dx_list = []
    embed_list = []
    hidden_list = []
    cot_list = []
    cot_full = cot_full_first
    for tick_index in range(tick_count):
        steps = steps_now[tick_index]
        count = counts_now[tick_index]
        embedded = lax.dynamic_index_in_dim(step_table, steps, keepdims=False).astype(
            jnp.float32
        )
        gain = 1.0 + lax.dynamic_slice_in_dim(embedded, chunk_start, chunk)
        bias = lax.dynamic_slice_in_dim(embedded, channels + chunk_start, chunk)
        mask = (jnp.arange(frames, dtype=jnp.int32) < count).astype(jnp.float32)
        mask_cells = mask[:, None, None, None]
        valid = count.astype(jnp.float32) * float(height_total * cells_wide * per_group)

        values = inputs_chunk[tick_index].astype(jnp.float32)
        masked = values * mask_cells
        mean_g = chunk_group_sums(masked, groups_here) / valid
        var_g = chunk_group_sums(masked * values, groups_here) / valid - mean_g * mean_g
        rstd_g = lax.rsqrt(var_g + EPS)
        mean_c = jnp.repeat(mean_g, per_group)
        rstd_c = jnp.repeat(rstd_g, per_group)
        normed = (values - mean_c) * rstd_c
        preact = normed * gain + bias
        hidden = (jax.nn.silu(preact) * mask_cells).astype(jnp.bfloat16)
        hidden_list.append(hidden)

        upward = lax.conv_general_dilated(
            cot_full[None],
            kernel,
            window_strides=(1, 1, 1),
            padding=((1, 1), (1, 1), (1, 1)),
            dimension_numbers=("NDHWC", "DHWIO", "NDHWC"),
            preferred_element_type=jnp.float32,
        )[0]
        pre_grad = upward * silu_grad(preact) * mask_cells
        dnormed = pre_grad * gain
        sum_a = chunk_group_sums(dnormed, groups_here) / valid
        sum_b = chunk_group_sums(dnormed * normed, groups_here) / valid
        scale_part = jnp.sum(pre_grad * normed, axis=(0, 1, 2))
        shift_part = jnp.sum(pre_grad, axis=(0, 1, 2))
        branch = (
            rstd_c
            * (dnormed - jnp.repeat(sum_a, per_group) - normed * jnp.repeat(sum_b, per_group))
            * mask_cells
        )
        cot_chunk = lax.dynamic_slice_in_dim(cot_full, chunk_start, chunk, axis=3)
        result = (cot_chunk.astype(jnp.float32) + branch).astype(jnp.bfloat16)
        embed_list.append(jnp.stack([scale_part, shift_part]))
        if tick_index + 1 < tick_count:
            result_full = jnp.transpose(
                gather_two_level(result, "slab", SLAB_INNER), (1, 2, 3, 0, 4)
            ).reshape(frames, height_total, cells_wide, channels)
        else:
            flat = result.size
            payload = jnp.concatenate(
                [result.astype(jnp.float32).reshape(-1), jnp.stack(embed_list).reshape(-1)]
            )
            collected = gather_two_level(payload, "slab", SLAB_INNER)
            result_full = jnp.transpose(
                collected[:, :flat].reshape((slab_count,) + result.shape), (1, 2, 3, 0, 4)
            ).reshape(frames, height_total, cells_wide, channels).astype(jnp.bfloat16)
            embed_all = jnp.transpose(
                collected[:, flat:].reshape(slab_count, tick_count, 2, chunk), (1, 2, 0, 3)
            )
        dx_list.append(
            lax.dynamic_slice_in_dim(result_full, slab_index * slab_rows, slab_rows, axis=1)
        )
        cot_list.append(cot_full)
        if tick_index + 1 < tick_count:
            received = lax.ppermute(result_full, "pipe", [(1, 0)])
            cot_full = jnp.where(section_index == 1, cot_full_later, received)

    embed_grad = embed_all.reshape(tick_count, 2 * channels) * embed_norm

    cot_all = jnp.stack(cot_list)
    hidden_all = jnp.pad(
        jnp.stack(hidden_list), ((0, 0), (1, 1), (1, 1), (1, 1), (0, 0))
    )
    hidden_taps = tap_stack(hidden_all, frames, height_total, cells_wide)
    grad_term = jnp.einsum(
        "kfrwo,tkfrwi->oti", cot_all, hidden_taps, preferred_element_type=jnp.float32
    )
    terms = (grad_term * weight_norm).astype(jnp.bfloat16)
    terms = terms.reshape(replicas, channels // replicas, taps, chunk)
    grad_shard = scatter_sum_two_level(terms, "dp", DP_INNER)
    weight_grad = gather_two_level(grad_shard.astype(jnp.bfloat16), "slab", SLAB_INNER)
    weight_grad = jnp.transpose(weight_grad, (1, 2, 0, 3)).astype(jnp.float32)
    weight_grad = weight_grad.reshape(weight_grad.shape[0], taps * channels)
    input_grads = jnp.stack(dx_list)[None, :, None]
    return (input_grads, weight_grad[None], embed_grad[None, :, None])


def solution(mesh):
    placed = (
        P("pipe", None, "dp", None, "slab", None, None),
        P(None, "dp", None, "slab", None, None),
        P("dp", None, "slab", None, None),
        P("pipe", "dp", None),
        P("pipe", None, None),
        P(None, "dp"),
        P(None, "dp"),
    )
    return jax.shard_map(
        local,
        mesh=mesh,
        in_specs=placed,
        out_specs=(
            P("pipe", None, "dp", None, "slab", None, None),
            P("pipe", "dp", None),
            P("pipe", None, "dp", None),
        ),
        check_vma=False,
    )
```

```python
import math

import jax
import jax.numpy as jnp
from jax import lax
from jax.sharding import PartitionSpec as P

GROUPS = 32

DP_INNER = 4
SLAB_INNER = 2


EPS = 1e-05


def silu_grad(preact):
    sigma = jax.nn.sigmoid(preact)
    return sigma * (1.0 + preact * (1.0 - sigma))


def chunk_group_sums(values, groups_here):
    summed = jnp.sum(values.reshape(-1, values.shape[-1]), axis=0)
    return jnp.sum(summed.reshape(groups_here, -1), axis=1)


def shifted_copies(value, axis):
    devices = lax.axis_size(axis)
    pieces = [value]
    for distance in range(1, devices):
        route = [(i, (i + distance) % devices) for i in range(devices)]
        pieces.append(lax.ppermute(value, axis, route))
    return pieces


def gather_stack(value, axis):
    devices = lax.axis_size(axis)
    here = lax.axis_index(axis)
    stacked = jnp.stack(shifted_copies(value, axis))
    order = (here - jnp.arange(devices, dtype=jnp.int32)) % devices
    return jnp.take(stacked, order, axis=0)


def exchange_blocks(blocks, axis):
    devices = lax.axis_size(axis)
    here = lax.axis_index(axis)
    pieces = [lax.dynamic_index_in_dim(blocks, here, keepdims=False)]
    for distance in range(1, devices):
        route = [(i, (i + distance) % devices) for i in range(devices)]
        target = (here + distance) % devices
        pieces.append(
            lax.ppermute(lax.dynamic_index_in_dim(blocks, target, keepdims=False), axis, route)
        )
    stacked = jnp.stack(pieces)
    order = (here - jnp.arange(devices, dtype=jnp.int32)) % devices
    return jnp.take(stacked, order, axis=0)


def scatter_sum(blocks, axis):
    devices = lax.axis_size(axis)
    here = lax.axis_index(axis)
    total = lax.dynamic_index_in_dim(blocks, here, keepdims=False).astype(jnp.float32)
    for distance in range(1, devices):
        route = [(i, (i + distance) % devices) for i in range(devices)]
        target = (here + distance) % devices
        sent = lax.dynamic_index_in_dim(blocks, target, keepdims=False)
        total = total + lax.ppermute(sent, axis, route).astype(jnp.float32)
    return total


def level_routes(devices, inner, along_low, distance):
    outer = devices // inner
    if along_low:
        return [(i, (i // inner) * inner + (i % inner + distance) % inner) for i in range(devices)]
    return [(i, ((i // inner + distance) % outer) * inner + i % inner) for i in range(devices)]


def gather_level(value, axis, inner, along_low):
    devices = lax.axis_size(axis)
    here = lax.axis_index(axis)
    count = inner if along_low else devices // inner
    position = here % inner if along_low else here // inner
    pieces = [value]
    for distance in range(1, count):
        pieces.append(lax.ppermute(value, axis, level_routes(devices, inner, along_low, distance)))
    order = (position - jnp.arange(count, dtype=jnp.int32)) % count
    return jnp.take(jnp.stack(pieces), order, axis=0)


def gather_two_level(value, axis, inner, low_first=True):
    devices = lax.axis_size(axis)
    first = gather_level(value, axis, inner, low_first)
    both = gather_level(first, axis, inner, not low_first)
    if not low_first:
        both = jnp.swapaxes(both, 0, 1)
    return both.reshape((devices,) + value.shape)


def scatter_level(grid, axis, inner, along_low, wire_type):
    devices = lax.axis_size(axis)
    here = lax.axis_index(axis)
    count = inner if along_low else devices // inner
    position = here % inner if along_low else here // inner
    total = lax.dynamic_index_in_dim(grid, position, keepdims=False).astype(jnp.float32)
    for distance in range(1, count):
        target = (position + distance) % count
        sent = lax.dynamic_index_in_dim(grid, target, keepdims=False).astype(wire_type)
        route = level_routes(devices, inner, along_low, distance)
        total = total + lax.ppermute(sent, axis, route).astype(jnp.float32)
    return total


def scatter_sum_two_level(blocks, axis, inner):
    devices = lax.axis_size(axis)
    outer = devices // inner
    grid = blocks.reshape((outer, inner) + blocks.shape[1:])
    partial = scatter_level(jnp.swapaxes(grid, 0, 1), axis, inner, True, blocks.dtype)
    return scatter_level(partial, axis, inner, False, jnp.bfloat16)


def tap_stack(padded, frames, rows, cells_wide):
    slices = []
    for depth_at in range(3):
        for vertical in range(3):
            for across in range(3):
                slices.append(
                    padded[
                        ...,
                        depth_at : depth_at + frames,
                        vertical : vertical + rows,
                        across : across + cells_wide,
                        :,
                    ]
                )
    return jnp.stack(slices, 0)


def local(
    saved_inputs, loss_cotangent, upstream, conv_weight, adagn_table, timesteps, frame_counts
):
    section_index = lax.axis_index("pipe")
    slab_index = lax.axis_index("slab")
    slab_count = lax.axis_size("slab")
    replicas = lax.axis_size("dp")
    inputs = saved_inputs[0, :, 0]
    tick_count, frames, slab_rows, cells_wide, channels = inputs.shape
    height_total = slab_rows * slab_count
    chunk = channels // slab_count
    per_group = channels // GROUPS
    groups_here = chunk // per_group
    step_table = adagn_table[0]
    taps = 27
    weight_local = conv_weight[0].reshape(-1, taps, channels)
    steps_now = lax.dynamic_slice_in_dim(timesteps[:, 0], section_index, tick_count)
    counts_now = lax.dynamic_slice_in_dim(frame_counts[:, 0], section_index, tick_count)
    chunk_start = slab_index * chunk

    weight_cols = lax.dynamic_slice_in_dim(weight_local, chunk_start, chunk, axis=2)
    weight_chunk = gather_two_level(weight_cols, "dp", DP_INNER, low_first=False)
    kernel = weight_chunk.reshape(channels, 3, 3, 3, chunk)[:, ::-1, ::-1, ::-1, :]
    kernel = jnp.transpose(kernel, (1, 2, 3, 0, 4))


    weight_norm = 1.0 / math.sqrt(tick_count * replicas * frames * height_total * cells_wide)
    embed_norm = 1.0 / math.sqrt(frames * height_total * cells_wide)

    cot_first = jnp.where(section_index == 1, loss_cotangent[0, 0], upstream[0])
    starting = jnp.concatenate([inputs, cot_first[None], loss_cotangent[1, 0][None]])
    gathered = gather_two_level(starting, "slab", SLAB_INNER)
    gathered = jnp.transpose(gathered, (1, 2, 0, 3, 4, 5)).reshape(
        2 * tick_count, frames, height_total, cells_wide, channels
    )
    inputs_chunk = lax.dynamic_slice_in_dim(gathered[:tick_count], chunk_start, chunk, axis=4)
    cot_both = gathered[tick_count:]
    cot_full_first = cot_both[0]
    cot_full_later = cot_both[1]

    dx_list = []
    embed_list = []
    hidden_list = []
    cot_list = []
    cot_full = cot_full_first
    for tick_index in range(tick_count):
        steps = steps_now[tick_index]
        count = counts_now[tick_index]
        embedded = lax.dynamic_index_in_dim(step_table, steps, keepdims=False).astype(
            jnp.float32
        )
        gain = 1.0 + lax.dynamic_slice_in_dim(embedded, chunk_start, chunk)
        bias = lax.dynamic_slice_in_dim(embedded, channels + chunk_start, chunk)
        mask = (jnp.arange(frames, dtype=jnp.int32) < count).astype(jnp.float32)
        mask_cells = mask[:, None, None, None]
        valid = count.astype(jnp.float32) * float(height_total * cells_wide * per_group)

        values = inputs_chunk[tick_index].astype(jnp.float32)
        masked = values * mask_cells
        mean_g = chunk_group_sums(masked, groups_here) / valid
        var_g = chunk_group_sums(masked * values, groups_here) / valid - mean_g * mean_g
        rstd_g = lax.rsqrt(var_g + EPS)
        mean_c = jnp.repeat(mean_g, per_group)
        rstd_c = jnp.repeat(rstd_g, per_group)
        normed = (values - mean_c) * rstd_c
        preact = normed * gain + bias
        hidden = (jax.nn.silu(preact) * mask_cells).astype(jnp.bfloat16)
        hidden_list.append(hidden)

        upward = lax.conv_general_dilated(
            cot_full[None],
            kernel,
            window_strides=(1, 1, 1),
            padding=((1, 1), (1, 1), (1, 1)),
            dimension_numbers=("NDHWC", "DHWIO", "NDHWC"),
            preferred_element_type=jnp.float32,
        )[0]
        pre_grad = upward * silu_grad(preact) * mask_cells
        dnormed = pre_grad * gain
        sum_a = chunk_group_sums(dnormed, groups_here) / valid
        sum_b = chunk_group_sums(dnormed * normed, groups_here) / valid
        scale_part = jnp.sum(pre_grad * normed, axis=(0, 1, 2))
        shift_part = jnp.sum(pre_grad, axis=(0, 1, 2))
        branch = (
            rstd_c
            * (dnormed - jnp.repeat(sum_a, per_group) - normed * jnp.repeat(sum_b, per_group))
            * mask_cells
        )
        cot_chunk = lax.dynamic_slice_in_dim(cot_full, chunk_start, chunk, axis=3)
        result = (cot_chunk.astype(jnp.float32) + branch).astype(jnp.bfloat16)
        embed_list.append(jnp.stack([scale_part, shift_part]))
        if tick_index + 1 < tick_count:
            result_full = jnp.transpose(
                gather_two_level(result, "slab", SLAB_INNER), (1, 2, 3, 0, 4)
            ).reshape(frames, height_total, cells_wide, channels)
        else:
            flat = result.size
            payload = jnp.concatenate(
                [result.astype(jnp.float32).reshape(-1), jnp.stack(embed_list).reshape(-1)]
            )
            collected = gather_two_level(payload, "slab", SLAB_INNER)
            result_full = jnp.transpose(
                collected[:, :flat].reshape((slab_count,) + result.shape), (1, 2, 3, 0, 4)
            ).reshape(frames, height_total, cells_wide, channels).astype(jnp.bfloat16)
            embed_all = jnp.transpose(
                collected[:, flat:].reshape(slab_count, tick_count, 2, chunk), (1, 2, 0, 3)
            )
        dx_list.append(
            lax.dynamic_slice_in_dim(result_full, slab_index * slab_rows, slab_rows, axis=1)
        )
        cot_list.append(cot_full)
        if tick_index + 1 < tick_count:
            received = lax.ppermute(result_full, "pipe", [(1, 0)])
            cot_full = jnp.where(section_index == 1, cot_full_later, received)

    embed_grad = embed_all.reshape(tick_count, 2 * channels) * embed_norm

    cot_all = jnp.stack(cot_list)
    hidden_all = jnp.pad(
        jnp.stack(hidden_list), ((0, 0), (1, 1), (1, 1), (1, 1), (0, 0))
    )
    hidden_taps = tap_stack(hidden_all, frames, height_total, cells_wide)
    grad_term = jnp.einsum(
        "kfrwo,tkfrwi->oti", cot_all, hidden_taps, preferred_element_type=jnp.float32
    )
    terms = (grad_term * weight_norm).astype(jnp.bfloat16)
    terms = terms.reshape(replicas, channels // replicas, taps, chunk)
    grad_shard = scatter_sum_two_level(terms, "dp", DP_INNER)
    weight_grad = gather_stack(grad_shard.astype(jnp.bfloat16), "slab")
    weight_grad = jnp.transpose(weight_grad, (1, 2, 0, 3)).astype(jnp.float32)
    weight_grad = weight_grad.reshape(weight_grad.shape[0], taps * channels)
    input_grads = jnp.stack(dx_list)[None, :, None]
    return (input_grads, weight_grad[None], embed_grad[None, :, None])


def solution(mesh):
    placed = (
        P("pipe", None, "dp", None, "slab", None, None),
        P(None, "dp", None, "slab", None, None),
        P("dp", None, "slab", None, None),
        P("pipe", "dp", None),
        P("pipe", None, None),
        P(None, "dp"),
        P(None, "dp"),
    )
    return jax.shard_map(
        local,
        mesh=mesh,
        in_specs=placed,
        out_specs=(
            P("pipe", None, "dp", None, "slab", None, None),
            P("pipe", "dp", None),
            P("pipe", None, "dp", None),
        ),
        check_vma=False,
    )
```

```python
import math

import jax
import jax.numpy as jnp
from jax import lax
from jax.sharding import PartitionSpec as P

GROUPS = 32

DP_INNER = 4
SLAB_INNER = 2


EPS = 1e-05


def silu_grad(preact):
    sigma = jax.nn.sigmoid(preact)
    return sigma * (1.0 + preact * (1.0 - sigma))


def chunk_group_sums(values, groups_here):
    summed = jnp.sum(values.reshape(-1, values.shape[-1]), axis=0)
    return jnp.sum(summed.reshape(groups_here, -1), axis=1)


def shifted_copies(value, axis):
    devices = lax.axis_size(axis)
    pieces = [value]
    for distance in range(1, devices):
        route = [(i, (i + distance) % devices) for i in range(devices)]
        pieces.append(lax.ppermute(value, axis, route))
    return pieces


def gather_stack(value, axis):
    devices = lax.axis_size(axis)
    here = lax.axis_index(axis)
    stacked = jnp.stack(shifted_copies(value, axis))
    order = (here - jnp.arange(devices, dtype=jnp.int32)) % devices
    return jnp.take(stacked, order, axis=0)


def exchange_blocks(blocks, axis):
    devices = lax.axis_size(axis)
    here = lax.axis_index(axis)
    pieces = [lax.dynamic_index_in_dim(blocks, here, keepdims=False)]
    for distance in range(1, devices):
        route = [(i, (i + distance) % devices) for i in range(devices)]
        target = (here + distance) % devices
        pieces.append(
            lax.ppermute(lax.dynamic_index_in_dim(blocks, target, keepdims=False), axis, route)
        )
    stacked = jnp.stack(pieces)
    order = (here - jnp.arange(devices, dtype=jnp.int32)) % devices
    return jnp.take(stacked, order, axis=0)


def scatter_sum(blocks, axis):
    devices = lax.axis_size(axis)
    here = lax.axis_index(axis)
    total = lax.dynamic_index_in_dim(blocks, here, keepdims=False).astype(jnp.float32)
    for distance in range(1, devices):
        route = [(i, (i + distance) % devices) for i in range(devices)]
        target = (here + distance) % devices
        sent = lax.dynamic_index_in_dim(blocks, target, keepdims=False)
        total = total + lax.ppermute(sent, axis, route).astype(jnp.float32)
    return total


def level_routes(devices, inner, along_low, distance):
    outer = devices // inner
    if along_low:
        return [(i, (i // inner) * inner + (i % inner + distance) % inner) for i in range(devices)]
    return [(i, ((i // inner + distance) % outer) * inner + i % inner) for i in range(devices)]


def gather_level(value, axis, inner, along_low):
    devices = lax.axis_size(axis)
    here = lax.axis_index(axis)
    count = inner if along_low else devices // inner
    position = here % inner if along_low else here // inner
    pieces = [value]
    for distance in range(1, count):
        pieces.append(lax.ppermute(value, axis, level_routes(devices, inner, along_low, distance)))
    placed = jnp.zeros((count,) + value.shape, value.dtype)
    for distance, piece in enumerate(pieces):
        placed = lax.dynamic_update_index_in_dim(placed, piece, (position - distance) % count, 0)
    return placed


def gather_two_level(value, axis, inner, low_first=True):
    devices = lax.axis_size(axis)
    first = gather_level(value, axis, inner, low_first)
    both = gather_level(first, axis, inner, not low_first)
    if not low_first:
        both = jnp.swapaxes(both, 0, 1)
    return both.reshape((devices,) + value.shape)


def scatter_level(grid, axis, inner, along_low, wire_type):
    devices = lax.axis_size(axis)
    here = lax.axis_index(axis)
    count = inner if along_low else devices // inner
    position = here % inner if along_low else here // inner
    total = lax.dynamic_index_in_dim(grid, position, keepdims=False).astype(jnp.float32)
    for distance in range(1, count):
        target = (position + distance) % count
        sent = lax.dynamic_index_in_dim(grid, target, keepdims=False).astype(wire_type)
        route = level_routes(devices, inner, along_low, distance)
        total = total + lax.ppermute(sent, axis, route).astype(jnp.float32)
    return total


def scatter_sum_two_level(blocks, axis, inner):
    devices = lax.axis_size(axis)
    outer = devices // inner
    grid = blocks.reshape((outer, inner) + blocks.shape[1:])
    partial = scatter_level(jnp.swapaxes(grid, 0, 1), axis, inner, True, blocks.dtype)
    return scatter_level(partial, axis, inner, False, jnp.bfloat16)


def tap_stack(padded, frames, rows, cells_wide):
    slices = []
    for depth_at in range(3):
        for vertical in range(3):
            for across in range(3):
                slices.append(
                    padded[
                        ...,
                        depth_at : depth_at + frames,
                        vertical : vertical + rows,
                        across : across + cells_wide,
                        :,
                    ]
                )
    return jnp.stack(slices, 0)


def local(
    saved_inputs, loss_cotangent, upstream, conv_weight, adagn_table, timesteps, frame_counts
):
    section_index = lax.axis_index("pipe")
    slab_index = lax.axis_index("slab")
    slab_count = lax.axis_size("slab")
    replicas = lax.axis_size("dp")
    inputs = saved_inputs[0, :, 0]
    tick_count, frames, slab_rows, cells_wide, channels = inputs.shape
    height_total = slab_rows * slab_count
    chunk = channels // slab_count
    per_group = channels // GROUPS
    groups_here = chunk // per_group
    step_table = adagn_table[0]
    taps = 27
    weight_local = conv_weight[0].reshape(-1, taps, channels)
    steps_now = lax.dynamic_slice_in_dim(timesteps[:, 0], section_index, tick_count)
    counts_now = lax.dynamic_slice_in_dim(frame_counts[:, 0], section_index, tick_count)
    chunk_start = slab_index * chunk

    weight_cols = lax.dynamic_slice_in_dim(weight_local, chunk_start, chunk, axis=2)
    weight_chunk = gather_two_level(weight_cols, "dp", DP_INNER, low_first=False)
    kernel = weight_chunk.reshape(channels, 3, 3, 3, chunk)[:, ::-1, ::-1, ::-1, :]
    kernel = jnp.transpose(kernel, (1, 2, 3, 0, 4))


    weight_norm = 1.0 / math.sqrt(tick_count * replicas * frames * height_total * cells_wide)
    embed_norm = 1.0 / math.sqrt(frames * height_total * cells_wide)

    cot_first = jnp.where(section_index == 1, loss_cotangent[0, 0], upstream[0])
    starting = jnp.concatenate([inputs, cot_first[None], loss_cotangent[1, 0][None]])
    gathered = gather_two_level(starting, "slab", SLAB_INNER)
    gathered = jnp.transpose(gathered, (1, 2, 0, 3, 4, 5)).reshape(
        2 * tick_count, frames, height_total, cells_wide, channels
    )
    inputs_chunk = lax.dynamic_slice_in_dim(gathered[:tick_count], chunk_start, chunk, axis=4)
    cot_both = gathered[tick_count:]
    cot_full_first = cot_both[0]
    cot_full_later = cot_both[1]

    dx_list = []
    embed_list = []
    hidden_list = []
    cot_list = []
    cot_full = cot_full_first
    for tick_index in range(tick_count):
        steps = steps_now[tick_index]
        count = counts_now[tick_index]
        embedded = lax.dynamic_index_in_dim(step_table, steps, keepdims=False).astype(
            jnp.float32
        )
        gain = 1.0 + lax.dynamic_slice_in_dim(embedded, chunk_start, chunk)
        bias = lax.dynamic_slice_in_dim(embedded, channels + chunk_start, chunk)
        mask = (jnp.arange(frames, dtype=jnp.int32) < count).astype(jnp.float32)
        mask_cells = mask[:, None, None, None]
        valid = count.astype(jnp.float32) * float(height_total * cells_wide * per_group)

        values = inputs_chunk[tick_index].astype(jnp.float32)
        masked = values * mask_cells
        mean_g = chunk_group_sums(masked, groups_here) / valid
        var_g = chunk_group_sums(masked * values, groups_here) / valid - mean_g * mean_g
        rstd_g = lax.rsqrt(var_g + EPS)
        mean_c = jnp.repeat(mean_g, per_group)
        rstd_c = jnp.repeat(rstd_g, per_group)
        normed = (values - mean_c) * rstd_c
        preact = normed * gain + bias
        hidden = (jax.nn.silu(preact) * mask_cells).astype(jnp.bfloat16)
        hidden_list.append(hidden)

        upward = lax.conv_general_dilated(
            cot_full[None],
            kernel,
            window_strides=(1, 1, 1),
            padding=((1, 1), (1, 1), (1, 1)),
            dimension_numbers=("NDHWC", "DHWIO", "NDHWC"),
            preferred_element_type=jnp.float32,
        )[0]
        pre_grad = upward * silu_grad(preact) * mask_cells
        dnormed = pre_grad * gain
        sum_a = chunk_group_sums(dnormed, groups_here) / valid
        sum_b = chunk_group_sums(dnormed * normed, groups_here) / valid
        scale_part = jnp.sum(pre_grad * normed, axis=(0, 1, 2))
        shift_part = jnp.sum(pre_grad, axis=(0, 1, 2))
        branch = (
            rstd_c
            * (dnormed - jnp.repeat(sum_a, per_group) - normed * jnp.repeat(sum_b, per_group))
            * mask_cells
        )
        cot_chunk = lax.dynamic_slice_in_dim(cot_full, chunk_start, chunk, axis=3)
        result = (cot_chunk.astype(jnp.float32) + branch).astype(jnp.bfloat16)
        embed_list.append(jnp.stack([scale_part, shift_part]))
        if tick_index + 1 < tick_count:
            result_full = jnp.transpose(
                gather_two_level(result, "slab", SLAB_INNER), (1, 2, 3, 0, 4)
            ).reshape(frames, height_total, cells_wide, channels)
        else:
            flat = result.size
            payload = jnp.concatenate(
                [result.astype(jnp.float32).reshape(-1), jnp.stack(embed_list).reshape(-1)]
            )
            collected = gather_two_level(payload, "slab", SLAB_INNER)
            result_full = jnp.transpose(
                collected[:, :flat].reshape((slab_count,) + result.shape), (1, 2, 3, 0, 4)
            ).reshape(frames, height_total, cells_wide, channels).astype(jnp.bfloat16)
            embed_all = jnp.transpose(
                collected[:, flat:].reshape(slab_count, tick_count, 2, chunk), (1, 2, 0, 3)
            )
        dx_list.append(
            lax.dynamic_slice_in_dim(result_full, slab_index * slab_rows, slab_rows, axis=1)
        )
        cot_list.append(cot_full)
        if tick_index + 1 < tick_count:
            received = lax.ppermute(result_full, "pipe", [(1, 0)])
            cot_full = jnp.where(section_index == 1, cot_full_later, received)

    embed_grad = embed_all.reshape(tick_count, 2 * channels) * embed_norm

    cot_all = jnp.stack(cot_list)
    hidden_all = jnp.pad(
        jnp.stack(hidden_list), ((0, 0), (1, 1), (1, 1), (1, 1), (0, 0))
    )
    hidden_taps = tap_stack(hidden_all, frames, height_total, cells_wide)
    grad_term = jnp.einsum(
        "kfrwo,tkfrwi->oti", cot_all, hidden_taps, preferred_element_type=jnp.float32
    )
    terms = (grad_term * weight_norm).astype(jnp.bfloat16)
    terms = terms.reshape(replicas, channels // replicas, taps, chunk)
    grad_shard = scatter_sum_two_level(terms, "dp", DP_INNER)
    weight_grad = gather_two_level(grad_shard.astype(jnp.bfloat16), "slab", SLAB_INNER)
    weight_grad = jnp.transpose(weight_grad, (1, 2, 0, 3)).astype(jnp.float32)
    weight_grad = weight_grad.reshape(weight_grad.shape[0], taps * channels)
    input_grads = jnp.stack(dx_list)[None, :, None]
    return (input_grads, weight_grad[None], embed_grad[None, :, None])


def solution(mesh):
    placed = (
        P("pipe", None, "dp", None, "slab", None, None),
        P(None, "dp", None, "slab", None, None),
        P("dp", None, "slab", None, None),
        P("pipe", "dp", None),
        P("pipe", None, None),
        P(None, "dp"),
        P(None, "dp"),
    )
    return jax.shard_map(
        local,
        mesh=mesh,
        in_specs=placed,
        out_specs=(
            P("pipe", None, "dp", None, "slab", None, None),
            P("pipe", "dp", None),
            P("pipe", None, "dp", None),
        ),
        check_vma=False,
    )
```

```python
import math

import jax
import jax.numpy as jnp
from jax import lax
from jax.sharding import PartitionSpec as P

GROUPS = 32

DP_INNER = 4
SLAB_INNER = 2


EPS = 1e-05


def silu_grad(preact):
    sigma = jax.nn.sigmoid(preact)
    return sigma * (1.0 + preact * (1.0 - sigma))


def chunk_group_sums(values, groups_here):
    summed = jnp.sum(values.reshape(-1, values.shape[-1]), axis=0)
    return jnp.sum(summed.reshape(groups_here, -1), axis=1)


def shifted_copies(value, axis):
    devices = lax.axis_size(axis)
    pieces = [value]
    for distance in range(1, devices):
        route = [(i, (i + distance) % devices) for i in range(devices)]
        pieces.append(lax.ppermute(value, axis, route))
    return pieces


def gather_stack(value, axis):
    devices = lax.axis_size(axis)
    here = lax.axis_index(axis)
    stacked = jnp.stack(shifted_copies(value, axis))
    order = (here - jnp.arange(devices, dtype=jnp.int32)) % devices
    return jnp.take(stacked, order, axis=0)


def exchange_blocks(blocks, axis):
    devices = lax.axis_size(axis)
    here = lax.axis_index(axis)
    pieces = [lax.dynamic_index_in_dim(blocks, here, keepdims=False)]
    for distance in range(1, devices):
        route = [(i, (i + distance) % devices) for i in range(devices)]
        target = (here + distance) % devices
        pieces.append(
            lax.ppermute(lax.dynamic_index_in_dim(blocks, target, keepdims=False), axis, route)
        )
    stacked = jnp.stack(pieces)
    order = (here - jnp.arange(devices, dtype=jnp.int32)) % devices
    return jnp.take(stacked, order, axis=0)


def scatter_sum(blocks, axis):
    devices = lax.axis_size(axis)
    here = lax.axis_index(axis)
    total = lax.dynamic_index_in_dim(blocks, here, keepdims=False).astype(jnp.float32)
    for distance in range(1, devices):
        route = [(i, (i + distance) % devices) for i in range(devices)]
        target = (here + distance) % devices
        sent = lax.dynamic_index_in_dim(blocks, target, keepdims=False)
        total = total + lax.ppermute(sent, axis, route).astype(jnp.float32)
    return total


def level_routes(devices, inner, along_low, distance):
    outer = devices // inner
    if along_low:
        return [(i, (i // inner) * inner + (i % inner + distance) % inner) for i in range(devices)]
    return [(i, ((i // inner + distance) % outer) * inner + i % inner) for i in range(devices)]


def gather_level(value, axis, inner, along_low):
    devices = lax.axis_size(axis)
    here = lax.axis_index(axis)
    count = inner if along_low else devices // inner
    position = here % inner if along_low else here // inner
    pieces = [value]
    for distance in range(1, count):
        pieces.append(lax.ppermute(value, axis, level_routes(devices, inner, along_low, distance)))
    placed = jnp.zeros((count,) + value.shape, value.dtype)
    for distance, piece in enumerate(pieces):
        placed = lax.dynamic_update_index_in_dim(placed, piece, (position - distance) % count, 0)
    return placed


def gather_two_level(value, axis, inner, low_first=True):
    devices = lax.axis_size(axis)
    first = gather_level(value, axis, inner, low_first)
    both = gather_level(first, axis, inner, not low_first)
    if not low_first:
        both = jnp.swapaxes(both, 0, 1)
    return both.reshape((devices,) + value.shape)


def scatter_level(grid, axis, inner, along_low, wire_type):
    devices = lax.axis_size(axis)
    here = lax.axis_index(axis)
    count = inner if along_low else devices // inner
    position = here % inner if along_low else here // inner
    total = lax.dynamic_index_in_dim(grid, position, keepdims=False).astype(jnp.float32)
    for distance in range(1, count):
        target = (position + distance) % count
        sent = lax.dynamic_index_in_dim(grid, target, keepdims=False).astype(wire_type)
        route = level_routes(devices, inner, along_low, distance)
        total = total + lax.ppermute(sent, axis, route).astype(jnp.float32)
    return total


def scatter_sum_two_level(blocks, axis, inner):
    devices = lax.axis_size(axis)
    outer = devices // inner
    grid = blocks.reshape((outer, inner) + blocks.shape[1:])
    partial = scatter_level(jnp.swapaxes(grid, 0, 1), axis, inner, True, blocks.dtype)
    return scatter_level(partial, axis, inner, False, jnp.bfloat16)


def tap_stack(padded, frames, rows, cells_wide):
    slices = []
    for depth_at in range(3):
        for vertical in range(3):
            for across in range(3):
                slices.append(
                    padded[
                        ...,
                        depth_at : depth_at + frames,
                        vertical : vertical + rows,
                        across : across + cells_wide,
                        :,
                    ]
                )
    return jnp.stack(slices, 0)


def local(
    saved_inputs, loss_cotangent, upstream, conv_weight, adagn_table, timesteps, frame_counts
):
    section_index = lax.axis_index("pipe")
    slab_index = lax.axis_index("slab")
    slab_count = lax.axis_size("slab")
    replicas = lax.axis_size("dp")
    inputs = saved_inputs[0, :, 0]
    tick_count, frames, slab_rows, cells_wide, channels = inputs.shape
    height_total = slab_rows * slab_count
    chunk = channels // slab_count
    per_group = channels // GROUPS
    groups_here = chunk // per_group
    step_table = adagn_table[0]
    taps = 27
    weight_local = conv_weight[0].reshape(-1, taps, channels)
    steps_now = lax.dynamic_slice_in_dim(timesteps[:, 0], section_index, tick_count)
    counts_now = lax.dynamic_slice_in_dim(frame_counts[:, 0], section_index, tick_count)
    chunk_start = slab_index * chunk

    weight_cols = lax.dynamic_slice_in_dim(weight_local, chunk_start, chunk, axis=2)
    weight_chunk = gather_two_level(weight_cols, "dp", DP_INNER, low_first=False)
    kernel = weight_chunk.reshape(channels, 3, 3, 3, chunk)[:, ::-1, ::-1, ::-1, :]
    kernel = jnp.transpose(kernel, (1, 2, 3, 0, 4))


    weight_norm = 1.0 / math.sqrt(tick_count * replicas * frames * height_total * cells_wide)
    embed_norm = 1.0 / math.sqrt(frames * height_total * cells_wide)

    cot_first = jnp.where(section_index == 1, loss_cotangent[0, 0], upstream[0])
    starting = jnp.concatenate([inputs, cot_first[None], loss_cotangent[1, 0][None]])
    gathered = gather_two_level(starting, "slab", SLAB_INNER)
    gathered = jnp.transpose(gathered, (1, 2, 0, 3, 4, 5)).reshape(
        2 * tick_count, frames, height_total, cells_wide, channels
    )
    inputs_chunk = lax.dynamic_slice_in_dim(gathered[:tick_count], chunk_start, chunk, axis=4)
    cot_both = gathered[tick_count:]
    cot_full_first = cot_both[0]
    cot_full_later = cot_both[1]

    dx_list = []
    embed_list = []
    hidden_list = []
    cot_list = []
    cot_full = cot_full_first
    for tick_index in range(tick_count):
        steps = steps_now[tick_index]
        count = counts_now[tick_index]
        embedded = lax.dynamic_index_in_dim(step_table, steps, keepdims=False).astype(
            jnp.float32
        )
        gain = 1.0 + lax.dynamic_slice_in_dim(embedded, chunk_start, chunk)
        bias = lax.dynamic_slice_in_dim(embedded, channels + chunk_start, chunk)
        mask = (jnp.arange(frames, dtype=jnp.int32) < count).astype(jnp.float32)
        mask_cells = mask[:, None, None, None]
        valid = count.astype(jnp.float32) * float(height_total * cells_wide * per_group)

        values = inputs_chunk[tick_index].astype(jnp.float32)
        masked = values * mask_cells
        mean_g = chunk_group_sums(masked, groups_here) / valid
        var_g = chunk_group_sums(masked * values, groups_here) / valid - mean_g * mean_g
        rstd_g = lax.rsqrt(var_g + EPS)
        mean_c = jnp.repeat(mean_g, per_group)
        rstd_c = jnp.repeat(rstd_g, per_group)
        normed = (values - mean_c) * rstd_c
        preact = normed * gain + bias
        hidden = (jax.nn.silu(preact) * mask_cells).astype(jnp.bfloat16)
        hidden_list.append(hidden)

        upward = lax.conv_general_dilated(
            cot_full[None],
            kernel,
            window_strides=(1, 1, 1),
            padding=((1, 1), (1, 1), (1, 1)),
            dimension_numbers=("NDHWC", "DHWIO", "NDHWC"),
            preferred_element_type=jnp.float32,
        )[0]
        pre_grad = upward * silu_grad(preact) * mask_cells
        dnormed = pre_grad * gain
        sum_a = chunk_group_sums(dnormed, groups_here) / valid
        sum_b = chunk_group_sums(dnormed * normed, groups_here) / valid
        scale_part = jnp.sum(pre_grad * normed, axis=(0, 1, 2))
        shift_part = jnp.sum(pre_grad, axis=(0, 1, 2))
        branch = (
            rstd_c
            * (dnormed - jnp.repeat(sum_a, per_group) - normed * jnp.repeat(sum_b, per_group))
            * mask_cells
        )
        cot_chunk = lax.dynamic_slice_in_dim(cot_full, chunk_start, chunk, axis=3)
        result = (cot_chunk.astype(jnp.float32) + branch).astype(jnp.bfloat16)
        embed_list.append(jnp.stack([scale_part, shift_part]))
        result_full = jnp.transpose(
            gather_two_level(result, "slab", SLAB_INNER), (1, 2, 3, 0, 4)
        ).reshape(frames, height_total, cells_wide, channels)
        dx_list.append(
            lax.dynamic_slice_in_dim(result_full, slab_index * slab_rows, slab_rows, axis=1)
        )
        cot_list.append(cot_full)
        if tick_index + 1 < tick_count:
            received = lax.ppermute(result_full, "pipe", [(1, 0)])
            cot_full = jnp.where(section_index == 1, cot_full_later, received)

    embed_all = jnp.transpose(
        gather_two_level(jnp.stack(embed_list), "slab", SLAB_INNER), (1, 2, 0, 3)
    )
    embed_grad = embed_all.reshape(tick_count, 2 * channels) * embed_norm

    cot_all = jnp.stack(cot_list)
    hidden_all = jnp.pad(
        jnp.stack(hidden_list), ((0, 0), (1, 1), (1, 1), (1, 1), (0, 0))
    )
    hidden_taps = tap_stack(hidden_all, frames, height_total, cells_wide)
    grad_term = jnp.einsum(
        "kfrwo,tkfrwi->oti", cot_all, hidden_taps, preferred_element_type=jnp.float32
    )
    terms = (grad_term * weight_norm).astype(jnp.bfloat16)
    terms = terms.reshape(replicas, channels // replicas, taps, chunk)
    grad_shard = scatter_sum_two_level(terms, "dp", DP_INNER)
    weight_grad = gather_two_level(grad_shard.astype(jnp.bfloat16), "slab", SLAB_INNER)
    weight_grad = jnp.transpose(weight_grad, (1, 2, 0, 3)).astype(jnp.float32)
    weight_grad = weight_grad.reshape(weight_grad.shape[0], taps * channels)
    input_grads = jnp.stack(dx_list)[None, :, None]
    return (input_grads, weight_grad[None], embed_grad[None, :, None])


def solution(mesh):
    placed = (
        P("pipe", None, "dp", None, "slab", None, None),
        P(None, "dp", None, "slab", None, None),
        P("dp", None, "slab", None, None),
        P("pipe", "dp", None),
        P("pipe", None, None),
        P(None, "dp"),
        P(None, "dp"),
    )
    return jax.shard_map(
        local,
        mesh=mesh,
        in_specs=placed,
        out_specs=(
            P("pipe", None, "dp", None, "slab", None, None),
            P("pipe", "dp", None),
            P("pipe", None, "dp", None),
        ),
        check_vma=False,
    )
```

```python
import math

import jax
import jax.numpy as jnp
from jax import lax
from jax.sharding import PartitionSpec as P

GROUPS = 32

DP_INNER = 4
SLAB_INNER = 2


EPS = 1e-05


def silu_grad(preact):
    sigma = jax.nn.sigmoid(preact)
    return sigma * (1.0 + preact * (1.0 - sigma))


def chunk_group_sums(values, groups_here):
    summed = jnp.sum(values.reshape(-1, values.shape[-1]), axis=0)
    return jnp.sum(summed.reshape(groups_here, -1), axis=1)


def shifted_copies(value, axis):
    devices = lax.axis_size(axis)
    pieces = [value]
    for distance in range(1, devices):
        route = [(i, (i + distance) % devices) for i in range(devices)]
        pieces.append(lax.ppermute(value, axis, route))
    return pieces


def gather_stack(value, axis):
    devices = lax.axis_size(axis)
    here = lax.axis_index(axis)
    stacked = jnp.stack(shifted_copies(value, axis))
    order = (here - jnp.arange(devices, dtype=jnp.int32)) % devices
    return jnp.take(stacked, order, axis=0)


def exchange_blocks(blocks, axis):
    devices = lax.axis_size(axis)
    here = lax.axis_index(axis)
    pieces = [lax.dynamic_index_in_dim(blocks, here, keepdims=False)]
    for distance in range(1, devices):
        route = [(i, (i + distance) % devices) for i in range(devices)]
        target = (here + distance) % devices
        pieces.append(
            lax.ppermute(lax.dynamic_index_in_dim(blocks, target, keepdims=False), axis, route)
        )
    stacked = jnp.stack(pieces)
    order = (here - jnp.arange(devices, dtype=jnp.int32)) % devices
    return jnp.take(stacked, order, axis=0)


def scatter_sum(blocks, axis):
    devices = lax.axis_size(axis)
    here = lax.axis_index(axis)
    total = lax.dynamic_index_in_dim(blocks, here, keepdims=False).astype(jnp.float32)
    for distance in range(1, devices):
        route = [(i, (i + distance) % devices) for i in range(devices)]
        target = (here + distance) % devices
        sent = lax.dynamic_index_in_dim(blocks, target, keepdims=False)
        total = total + lax.ppermute(sent, axis, route).astype(jnp.float32)
    return total


def level_routes(devices, inner, along_low, distance):
    outer = devices // inner
    if along_low:
        return [(i, (i // inner) * inner + (i % inner + distance) % inner) for i in range(devices)]
    return [(i, ((i // inner + distance) % outer) * inner + i % inner) for i in range(devices)]


def gather_level(value, axis, inner, along_low):
    devices = lax.axis_size(axis)
    here = lax.axis_index(axis)
    count = inner if along_low else devices // inner
    position = here % inner if along_low else here // inner
    pieces = [value]
    for distance in range(1, count):
        pieces.append(lax.ppermute(value, axis, level_routes(devices, inner, along_low, distance)))
    placed = jnp.zeros((count,) + value.shape, value.dtype)
    for distance, piece in enumerate(pieces):
        placed = lax.dynamic_update_index_in_dim(placed, piece, (position - distance) % count, 0)
    return placed


def gather_two_level(value, axis, inner, low_first=True):
    devices = lax.axis_size(axis)
    first = gather_level(value, axis, inner, low_first)
    both = gather_level(first, axis, inner, not low_first)
    if not low_first:
        both = jnp.swapaxes(both, 0, 1)
    return both.reshape((devices,) + value.shape)


def scatter_level(grid, axis, inner, along_low, wire_type):
    devices = lax.axis_size(axis)
    here = lax.axis_index(axis)
    count = inner if along_low else devices // inner
    position = here % inner if along_low else here // inner
    total = lax.dynamic_index_in_dim(grid, position, keepdims=False).astype(jnp.float32)
    for distance in range(1, count):
        target = (position + distance) % count
        sent = lax.dynamic_index_in_dim(grid, target, keepdims=False).astype(wire_type)
        route = level_routes(devices, inner, along_low, distance)
        total = total + lax.ppermute(sent, axis, route).astype(jnp.float32)
    return total


def scatter_sum_two_level(blocks, axis, inner):
    devices = lax.axis_size(axis)
    outer = devices // inner
    grid = blocks.reshape((outer, inner) + blocks.shape[1:])
    partial = scatter_level(jnp.swapaxes(grid, 0, 1), axis, inner, True, blocks.dtype)
    return scatter_level(partial, axis, inner, False, jnp.bfloat16)


def tap_stack(padded, frames, rows, cells_wide):
    slices = []
    for depth_at in range(3):
        for vertical in range(3):
            for across in range(3):
                slices.append(
                    padded[
                        ...,
                        depth_at : depth_at + frames,
                        vertical : vertical + rows,
                        across : across + cells_wide,
                        :,
                    ]
                )
    return jnp.stack(slices, 0)


def local(
    saved_inputs, loss_cotangent, upstream, conv_weight, adagn_table, timesteps, frame_counts
):
    section_index = lax.axis_index("pipe")
    slab_index = lax.axis_index("slab")
    slab_count = lax.axis_size("slab")
    replicas = lax.axis_size("dp")
    inputs = saved_inputs[0, :, 0]
    tick_count, frames, slab_rows, cells_wide, channels = inputs.shape
    height_total = slab_rows * slab_count
    chunk = channels // slab_count
    per_group = channels // GROUPS
    groups_here = chunk // per_group
    step_table = adagn_table[0]
    taps = 27
    weight_local = conv_weight[0].reshape(-1, taps, channels)
    steps_now = lax.dynamic_slice_in_dim(timesteps[:, 0], section_index, tick_count)
    counts_now = lax.dynamic_slice_in_dim(frame_counts[:, 0], section_index, tick_count)
    chunk_start = slab_index * chunk

    weight_cols = lax.dynamic_slice_in_dim(weight_local, chunk_start, chunk, axis=2)
    weight_chunk = gather_two_level(weight_cols, "dp", DP_INNER, low_first=False)
    kernel = weight_chunk.reshape(channels, 3, 3, 3, chunk)[:, ::-1, ::-1, ::-1, :]
    kernel = jnp.transpose(kernel, (1, 2, 3, 0, 4))


    weight_norm = 1.0 / math.sqrt(tick_count * replicas * frames * height_total * cells_wide)
    embed_norm = 1.0 / math.sqrt(frames * height_total * cells_wide)

    cot_first = jnp.where(section_index == 1, loss_cotangent[0, 0], upstream[0])
    starting = jnp.concatenate([inputs, cot_first[None], loss_cotangent[1, 0][None]])
    gathered = gather_two_level(starting, "slab", SLAB_INNER)
    gathered = jnp.transpose(gathered, (1, 2, 0, 3, 4, 5)).reshape(
        2 * tick_count, frames, height_total, cells_wide, channels
    )
    inputs_chunk = lax.dynamic_slice_in_dim(gathered[:tick_count], chunk_start, chunk, axis=4)
    cot_both = gathered[tick_count:]
    cot_full_first = cot_both[0]
    cot_full_later = cot_both[1]

    dx_list = []
    embed_list = []
    hidden_list = []
    cot_list = []
    cot_full = cot_full_first
    for tick_index in range(tick_count):
        steps = steps_now[tick_index]
        count = counts_now[tick_index]
        embedded = lax.dynamic_index_in_dim(step_table, steps, keepdims=False).astype(
            jnp.float32
        )
        gain = 1.0 + lax.dynamic_slice_in_dim(embedded, chunk_start, chunk)
        bias = lax.dynamic_slice_in_dim(embedded, channels + chunk_start, chunk)
        mask = (jnp.arange(frames, dtype=jnp.int32) < count).astype(jnp.float32)
        mask_cells = mask[:, None, None, None]
        valid = count.astype(jnp.float32) * float(height_total * cells_wide * per_group)

        values = inputs_chunk[tick_index].astype(jnp.float32)
        masked = values * mask_cells
        mean_g = chunk_group_sums(masked, groups_here) / valid
        var_g = chunk_group_sums(masked * values, groups_here) / valid - mean_g * mean_g
        rstd_g = lax.rsqrt(var_g + EPS)
        mean_c = jnp.repeat(mean_g, per_group)
        rstd_c = jnp.repeat(rstd_g, per_group)
        normed = (values - mean_c) * rstd_c
        preact = normed * gain + bias
        hidden = (jax.nn.silu(preact) * mask_cells).astype(jnp.bfloat16)
        hidden_list.append(hidden)

        upward = lax.conv_general_dilated(
            cot_full[None],
            kernel,
            window_strides=(1, 1, 1),
            padding=((1, 1), (1, 1), (1, 1)),
            dimension_numbers=("NDHWC", "DHWIO", "NDHWC"),
            preferred_element_type=jnp.float32,
        )[0]
        pre_grad = upward * silu_grad(preact) * mask_cells
        dnormed = pre_grad * gain
        sum_a = chunk_group_sums(dnormed, groups_here) / valid
        sum_b = chunk_group_sums(dnormed * normed, groups_here) / valid
        scale_part = jnp.sum(pre_grad * normed, axis=(0, 1, 2))
        shift_part = jnp.sum(pre_grad, axis=(0, 1, 2))
        branch = (
            rstd_c
            * (dnormed - jnp.repeat(sum_a, per_group) - normed * jnp.repeat(sum_b, per_group))
            * mask_cells
        )
        cot_chunk = lax.dynamic_slice_in_dim(cot_full, chunk_start, chunk, axis=3)
        result = (cot_chunk.astype(jnp.float32) + branch).astype(jnp.bfloat16)
        embed_list.append(jnp.stack([scale_part, shift_part]))
        result_full = jnp.transpose(
            gather_two_level(result, "slab", SLAB_INNER), (1, 2, 3, 0, 4)
        ).reshape(frames, height_total, cells_wide, channels)
        dx_list.append(
            lax.dynamic_slice_in_dim(result_full, slab_index * slab_rows, slab_rows, axis=1)
        )
        cot_list.append(cot_full)
        if tick_index + 1 < tick_count:
            received = lax.ppermute(result_full, "pipe", [(1, 0)])
            cot_full = jnp.where(section_index == 1, cot_full_later, received)

    embed_all = jnp.transpose(
        gather_two_level(jnp.stack(embed_list), "slab", SLAB_INNER), (1, 2, 0, 3)
    )
    embed_grad = embed_all.reshape(tick_count, 2 * channels) * embed_norm

    cot_all = jnp.stack(cot_list)
    hidden_all = jnp.pad(
        jnp.stack(hidden_list), ((0, 0), (1, 1), (1, 1), (1, 1), (0, 0))
    )
    hidden_taps = tap_stack(hidden_all, frames, height_total, cells_wide)
    cot_split = cot_all.reshape(
        cot_all.shape[:-1] + (replicas // DP_INNER, DP_INNER, channels // replicas)
    )
    grad_term = jnp.einsum(
        "kfrwzyo,tkfrwi->yzoti", cot_split, hidden_taps, preferred_element_type=jnp.float32
    )
    terms = (grad_term * weight_norm).astype(jnp.bfloat16)
    partial = scatter_level(terms, "dp", DP_INNER, True, terms.dtype)
    grad_shard = scatter_level(partial, "dp", DP_INNER, False, jnp.bfloat16)
    weight_grad = gather_two_level(grad_shard.astype(jnp.bfloat16), "slab", SLAB_INNER)
    weight_grad = jnp.transpose(weight_grad, (1, 2, 0, 3)).astype(jnp.float32)
    weight_grad = weight_grad.reshape(weight_grad.shape[0], taps * channels)
    input_grads = jnp.stack(dx_list)[None, :, None]
    return (input_grads, weight_grad[None], embed_grad[None, :, None])


def solution(mesh):
    placed = (
        P("pipe", None, "dp", None, "slab", None, None),
        P(None, "dp", None, "slab", None, None),
        P("dp", None, "slab", None, None),
        P("pipe", "dp", None),
        P("pipe", None, None),
        P(None, "dp"),
        P(None, "dp"),
    )
    return jax.shard_map(
        local,
        mesh=mesh,
        in_specs=placed,
        out_specs=(
            P("pipe", None, "dp", None, "slab", None, None),
            P("pipe", "dp", None),
            P("pipe", None, "dp", None),
        ),
        check_vma=False,
    )
```

```python
import math

import jax
import jax.numpy as jnp
from jax import lax
from jax.sharding import PartitionSpec as P

GROUPS = 32

DP_INNER = 4
SLAB_INNER = 2


EPS = 1e-05


def silu_grad(preact):
    sigma = jax.nn.sigmoid(preact)
    return sigma * (1.0 + preact * (1.0 - sigma))


def chunk_group_sums(values, groups_here):
    summed = jnp.sum(values.reshape(-1, values.shape[-1]), axis=0)
    return jnp.sum(summed.reshape(groups_here, -1), axis=1)


def shifted_copies(value, axis):
    devices = lax.axis_size(axis)
    pieces = [value]
    for distance in range(1, devices):
        route = [(i, (i + distance) % devices) for i in range(devices)]
        pieces.append(lax.ppermute(value, axis, route))
    return pieces


def gather_stack(value, axis):
    devices = lax.axis_size(axis)
    here = lax.axis_index(axis)
    stacked = jnp.stack(shifted_copies(value, axis))
    order = (here - jnp.arange(devices, dtype=jnp.int32)) % devices
    return jnp.take(stacked, order, axis=0)


def exchange_blocks(blocks, axis):
    devices = lax.axis_size(axis)
    here = lax.axis_index(axis)
    pieces = [lax.dynamic_index_in_dim(blocks, here, keepdims=False)]
    for distance in range(1, devices):
        route = [(i, (i + distance) % devices) for i in range(devices)]
        target = (here + distance) % devices
        pieces.append(
            lax.ppermute(lax.dynamic_index_in_dim(blocks, target, keepdims=False), axis, route)
        )
    stacked = jnp.stack(pieces)
    order = (here - jnp.arange(devices, dtype=jnp.int32)) % devices
    return jnp.take(stacked, order, axis=0)


def scatter_sum(blocks, axis):
    devices = lax.axis_size(axis)
    here = lax.axis_index(axis)
    total = lax.dynamic_index_in_dim(blocks, here, keepdims=False).astype(jnp.float32)
    for distance in range(1, devices):
        route = [(i, (i + distance) % devices) for i in range(devices)]
        target = (here + distance) % devices
        sent = lax.dynamic_index_in_dim(blocks, target, keepdims=False)
        total = total + lax.ppermute(sent, axis, route).astype(jnp.float32)
    return total


def level_routes(devices, inner, along_low, distance):
    outer = devices // inner
    if along_low:
        return [(i, (i // inner) * inner + (i % inner + distance) % inner) for i in range(devices)]
    return [(i, ((i // inner + distance) % outer) * inner + i % inner) for i in range(devices)]


def gather_level(value, axis, inner, along_low):
    devices = lax.axis_size(axis)
    here = lax.axis_index(axis)
    count = inner if along_low else devices // inner
    position = here % inner if along_low else here // inner
    pieces = [value]
    for distance in range(1, count):
        pieces.append(lax.ppermute(value, axis, level_routes(devices, inner, along_low, distance)))
    placed = jnp.zeros((count,) + value.shape, value.dtype)
    for distance, piece in enumerate(pieces):
        placed = lax.dynamic_update_index_in_dim(placed, piece, (position - distance) % count, 0)
    return placed


def gather_level_into(value, axis, inner, along_low, dim):
    devices = lax.axis_size(axis)
    here = lax.axis_index(axis)
    count = inner if along_low else devices // inner
    position = here % inner if along_low else here // inner
    pieces = [value]
    for distance in range(1, count):
        pieces.append(lax.ppermute(value, axis, level_routes(devices, inner, along_low, distance)))
    placed = jnp.zeros(value.shape[:dim] + (count,) + value.shape[dim:], value.dtype)
    for distance, piece in enumerate(pieces):
        placed = lax.dynamic_update_index_in_dim(placed, piece, (position - distance) % count, dim)
    return placed


def gather_two_level(value, axis, inner, low_first=True):
    devices = lax.axis_size(axis)
    first = gather_level(value, axis, inner, low_first)
    both = gather_level(first, axis, inner, not low_first)
    if not low_first:
        both = jnp.swapaxes(both, 0, 1)
    return both.reshape((devices,) + value.shape)


def scatter_level(grid, axis, inner, along_low, wire_type):
    devices = lax.axis_size(axis)
    here = lax.axis_index(axis)
    count = inner if along_low else devices // inner
    position = here % inner if along_low else here // inner
    total = lax.dynamic_index_in_dim(grid, position, keepdims=False).astype(jnp.float32)
    for distance in range(1, count):
        target = (position + distance) % count
        sent = lax.dynamic_index_in_dim(grid, target, keepdims=False).astype(wire_type)
        route = level_routes(devices, inner, along_low, distance)
        total = total + lax.ppermute(sent, axis, route).astype(jnp.float32)
    return total


def scatter_sum_two_level(blocks, axis, inner):
    devices = lax.axis_size(axis)
    outer = devices // inner
    grid = blocks.reshape((outer, inner) + blocks.shape[1:])
    partial = scatter_level(jnp.swapaxes(grid, 0, 1), axis, inner, True, blocks.dtype)
    return scatter_level(partial, axis, inner, False, jnp.bfloat16)


def tap_stack(padded, frames, rows, cells_wide):
    slices = []
    for depth_at in range(3):
        for vertical in range(3):
            for across in range(3):
                slices.append(
                    padded[
                        ...,
                        depth_at : depth_at + frames,
                        vertical : vertical + rows,
                        across : across + cells_wide,
                        :,
                    ]
                )
    return jnp.stack(slices, 0)


def local(
    saved_inputs, loss_cotangent, upstream, conv_weight, adagn_table, timesteps, frame_counts
):
    section_index = lax.axis_index("pipe")
    slab_index = lax.axis_index("slab")
    slab_count = lax.axis_size("slab")
    replicas = lax.axis_size("dp")
    inputs = saved_inputs[0, :, 0]
    tick_count, frames, slab_rows, cells_wide, channels = inputs.shape
    height_total = slab_rows * slab_count
    chunk = channels // slab_count
    per_group = channels // GROUPS
    groups_here = chunk // per_group
    step_table = adagn_table[0]
    taps = 27
    weight_local = conv_weight[0].reshape(-1, taps, channels)
    steps_now = lax.dynamic_slice_in_dim(timesteps[:, 0], section_index, tick_count)
    counts_now = lax.dynamic_slice_in_dim(frame_counts[:, 0], section_index, tick_count)
    chunk_start = slab_index * chunk

    weight_cols = lax.dynamic_slice_in_dim(weight_local, chunk_start, chunk, axis=2)
    weight_chunk = gather_two_level(weight_cols, "dp", DP_INNER, low_first=False)
    kernel = weight_chunk.reshape(channels, 3, 3, 3, chunk)[:, ::-1, ::-1, ::-1, :]
    kernel = jnp.transpose(kernel, (1, 2, 3, 0, 4))


    weight_norm = 1.0 / math.sqrt(tick_count * replicas * frames * height_total * cells_wide)
    embed_norm = 1.0 / math.sqrt(frames * height_total * cells_wide)

    cot_first = jnp.where(section_index == 1, loss_cotangent[0, 0], upstream[0])
    starting = jnp.concatenate([inputs, cot_first[None], loss_cotangent[1, 0][None]])
    gathered = gather_two_level(starting, "slab", SLAB_INNER)
    gathered = jnp.transpose(gathered, (1, 2, 0, 3, 4, 5)).reshape(
        2 * tick_count, frames, height_total, cells_wide, channels
    )
    inputs_chunk = lax.dynamic_slice_in_dim(gathered[:tick_count], chunk_start, chunk, axis=4)
    cot_both = gathered[tick_count:]
    cot_full_first = cot_both[0]
    cot_full_later = cot_both[1]

    dx_list = []
    embed_list = []
    hidden_list = []
    cot_list = []
    cot_full = cot_full_first
    for tick_index in range(tick_count):
        steps = steps_now[tick_index]
        count = counts_now[tick_index]
        embedded = lax.dynamic_index_in_dim(step_table, steps, keepdims=False).astype(
            jnp.float32
        )
        gain = 1.0 + lax.dynamic_slice_in_dim(embedded, chunk_start, chunk)
        bias = lax.dynamic_slice_in_dim(embedded, channels + chunk_start, chunk)
        mask = (jnp.arange(frames, dtype=jnp.int32) < count).astype(jnp.float32)
        mask_cells = mask[:, None, None, None]
        valid = count.astype(jnp.float32) * float(height_total * cells_wide * per_group)

        values = inputs_chunk[tick_index].astype(jnp.float32)
        masked = values * mask_cells
        mean_g = chunk_group_sums(masked, groups_here) / valid
        var_g = chunk_group_sums(masked * values, groups_here) / valid - mean_g * mean_g
        rstd_g = lax.rsqrt(var_g + EPS)
        mean_c = jnp.repeat(mean_g, per_group)
        rstd_c = jnp.repeat(rstd_g, per_group)
        normed = (values - mean_c) * rstd_c
        preact = normed * gain + bias
        hidden = (jax.nn.silu(preact) * mask_cells).astype(jnp.bfloat16)
        hidden_list.append(hidden)

        upward = lax.conv_general_dilated(
            cot_full[None],
            kernel,
            window_strides=(1, 1, 1),
            padding=((1, 1), (1, 1), (1, 1)),
            dimension_numbers=("NDHWC", "DHWIO", "NDHWC"),
            preferred_element_type=jnp.float32,
        )[0]
        pre_grad = upward * silu_grad(preact) * mask_cells
        dnormed = pre_grad * gain
        sum_a = chunk_group_sums(dnormed, groups_here) / valid
        sum_b = chunk_group_sums(dnormed * normed, groups_here) / valid
        scale_part = jnp.sum(pre_grad * normed, axis=(0, 1, 2))
        shift_part = jnp.sum(pre_grad, axis=(0, 1, 2))
        branch = (
            rstd_c
            * (dnormed - jnp.repeat(sum_a, per_group) - normed * jnp.repeat(sum_b, per_group))
            * mask_cells
        )
        cot_chunk = lax.dynamic_slice_in_dim(cot_full, chunk_start, chunk, axis=3)
        result = (cot_chunk.astype(jnp.float32) + branch).astype(jnp.bfloat16)
        embed_list.append(jnp.stack([scale_part, shift_part]))
        result_full = jnp.transpose(
            gather_two_level(result, "slab", SLAB_INNER), (1, 2, 3, 0, 4)
        ).reshape(frames, height_total, cells_wide, channels)
        dx_list.append(
            lax.dynamic_slice_in_dim(result_full, slab_index * slab_rows, slab_rows, axis=1)
        )
        cot_list.append(cot_full)
        if tick_index + 1 < tick_count:
            received = lax.ppermute(result_full, "pipe", [(1, 0)])
            cot_full = jnp.where(section_index == 1, cot_full_later, received)

    embed_all = jnp.transpose(
        gather_two_level(jnp.stack(embed_list), "slab", SLAB_INNER), (1, 2, 0, 3)
    )
    embed_grad = embed_all.reshape(tick_count, 2 * channels) * embed_norm

    cot_all = jnp.stack(cot_list)
    hidden_all = jnp.pad(
        jnp.stack(hidden_list), ((0, 0), (1, 1), (1, 1), (1, 1), (0, 0))
    )
    hidden_taps = tap_stack(hidden_all, frames, height_total, cells_wide)
    grad_term = jnp.einsum(
        "kfrwo,tkfrwi->oti", cot_all, hidden_taps, preferred_element_type=jnp.float32
    )
    terms = (grad_term * weight_norm).astype(jnp.bfloat16)
    terms = terms.reshape(replicas, channels // replicas, taps, chunk)
    grad_shard = scatter_sum_two_level(terms, "dp", DP_INNER)
    weight_grad = gather_level_into(grad_shard.astype(jnp.bfloat16), "slab", SLAB_INNER, True, 2)
    weight_grad = gather_level_into(weight_grad, "slab", SLAB_INNER, False, 2)
    weight_grad = weight_grad.reshape(weight_grad.shape[0], taps * channels).astype(jnp.float32)
    input_grads = jnp.stack(dx_list)[None, :, None]
    return (input_grads, weight_grad[None], embed_grad[None, :, None])


def solution(mesh):
    placed = (
        P("pipe", None, "dp", None, "slab", None, None),
        P(None, "dp", None, "slab", None, None),
        P("dp", None, "slab", None, None),
        P("pipe", "dp", None),
        P("pipe", None, None),
        P(None, "dp"),
        P(None, "dp"),
    )
    return jax.shard_map(
        local,
        mesh=mesh,
        in_specs=placed,
        out_specs=(
            P("pipe", None, "dp", None, "slab", None, None),
            P("pipe", "dp", None),
            P("pipe", None, "dp", None),
        ),
        check_vma=False,
    )
```

```python
import math

import jax
import jax.numpy as jnp
from jax import lax
from jax.sharding import PartitionSpec as P

GROUPS = 32

DP_INNER = 4
SLAB_INNER = 2


EPS = 1e-05


def silu_grad(preact):
    sigma = jax.nn.sigmoid(preact)
    return sigma * (1.0 + preact * (1.0 - sigma))


def chunk_group_sums(values, groups_here):
    summed = jnp.sum(values.reshape(-1, values.shape[-1]), axis=0)
    return jnp.sum(summed.reshape(groups_here, -1), axis=1)


def shifted_copies(value, axis):
    devices = lax.axis_size(axis)
    pieces = [value]
    for distance in range(1, devices):
        route = [(i, (i + distance) % devices) for i in range(devices)]
        pieces.append(lax.ppermute(value, axis, route))
    return pieces


def gather_stack(value, axis):
    devices = lax.axis_size(axis)
    here = lax.axis_index(axis)
    stacked = jnp.stack(shifted_copies(value, axis))
    order = (here - jnp.arange(devices, dtype=jnp.int32)) % devices
    return jnp.take(stacked, order, axis=0)


def exchange_blocks(blocks, axis):
    devices = lax.axis_size(axis)
    here = lax.axis_index(axis)
    pieces = [lax.dynamic_index_in_dim(blocks, here, keepdims=False)]
    for distance in range(1, devices):
        route = [(i, (i + distance) % devices) for i in range(devices)]
        target = (here + distance) % devices
        pieces.append(
            lax.ppermute(lax.dynamic_index_in_dim(blocks, target, keepdims=False), axis, route)
        )
    stacked = jnp.stack(pieces)
    order = (here - jnp.arange(devices, dtype=jnp.int32)) % devices
    return jnp.take(stacked, order, axis=0)


def scatter_sum(blocks, axis):
    devices = lax.axis_size(axis)
    here = lax.axis_index(axis)
    total = lax.dynamic_index_in_dim(blocks, here, keepdims=False).astype(jnp.float32)
    for distance in range(1, devices):
        route = [(i, (i + distance) % devices) for i in range(devices)]
        target = (here + distance) % devices
        sent = lax.dynamic_index_in_dim(blocks, target, keepdims=False)
        total = total + lax.ppermute(sent, axis, route).astype(jnp.float32)
    return total


def level_routes(devices, inner, along_low, distance):
    outer = devices // inner
    if along_low:
        return [(i, (i // inner) * inner + (i % inner + distance) % inner) for i in range(devices)]
    return [(i, ((i // inner + distance) % outer) * inner + i % inner) for i in range(devices)]


def gather_level(value, axis, inner, along_low):
    devices = lax.axis_size(axis)
    here = lax.axis_index(axis)
    count = inner if along_low else devices // inner
    position = here % inner if along_low else here // inner
    pieces = [value]
    for distance in range(1, count):
        pieces.append(lax.ppermute(value, axis, level_routes(devices, inner, along_low, distance)))
    placed = jnp.zeros((count,) + value.shape, value.dtype)
    for distance, piece in enumerate(pieces):
        placed = lax.dynamic_update_index_in_dim(placed, piece, (position - distance) % count, 0)
    return placed


def gather_level_into(value, axis, inner, along_low, dim):
    devices = lax.axis_size(axis)
    here = lax.axis_index(axis)
    count = inner if along_low else devices // inner
    position = here % inner if along_low else here // inner
    pieces = [value]
    for distance in range(1, count):
        pieces.append(lax.ppermute(value, axis, level_routes(devices, inner, along_low, distance)))
    placed = jnp.zeros(value.shape[:dim] + (count,) + value.shape[dim:], value.dtype)
    for distance, piece in enumerate(pieces):
        placed = lax.dynamic_update_index_in_dim(placed, piece, (position - distance) % count, dim)
    return placed


def gather_two_level(value, axis, inner, low_first=True):
    devices = lax.axis_size(axis)
    first = gather_level(value, axis, inner, low_first)
    both = gather_level(first, axis, inner, not low_first)
    if not low_first:
        both = jnp.swapaxes(both, 0, 1)
    return both.reshape((devices,) + value.shape)


def scatter_level(grid, axis, inner, along_low, wire_type):
    devices = lax.axis_size(axis)
    here = lax.axis_index(axis)
    count = inner if along_low else devices // inner
    position = here % inner if along_low else here // inner
    total = lax.dynamic_index_in_dim(grid, position, keepdims=False).astype(jnp.float32)
    for distance in range(1, count):
        target = (position + distance) % count
        sent = lax.dynamic_index_in_dim(grid, target, keepdims=False).astype(wire_type)
        route = level_routes(devices, inner, along_low, distance)
        total = total + lax.ppermute(sent, axis, route).astype(jnp.float32)
    return total


def scatter_sum_two_level(blocks, axis, inner):
    devices = lax.axis_size(axis)
    outer = devices // inner
    grid = blocks.reshape((outer, inner) + blocks.shape[1:])
    partial = scatter_level(jnp.swapaxes(grid, 0, 1), axis, inner, True, blocks.dtype)
    return scatter_level(partial, axis, inner, False, jnp.bfloat16)


def tap_stack(padded, frames, rows, cells_wide):
    slices = []
    for depth_at in range(3):
        for vertical in range(3):
            for across in range(3):
                slices.append(
                    padded[
                        ...,
                        depth_at : depth_at + frames,
                        vertical : vertical + rows,
                        across : across + cells_wide,
                        :,
                    ]
                )
    return jnp.stack(slices, 0)


def local(
    saved_inputs, loss_cotangent, upstream, conv_weight, adagn_table, timesteps, frame_counts
):
    section_index = lax.axis_index("pipe")
    slab_index = lax.axis_index("slab")
    slab_count = lax.axis_size("slab")
    replicas = lax.axis_size("dp")
    inputs = saved_inputs[0, :, 0]
    tick_count, frames, slab_rows, cells_wide, channels = inputs.shape
    height_total = slab_rows * slab_count
    chunk = channels // slab_count
    per_group = channels // GROUPS
    groups_here = chunk // per_group
    step_table = adagn_table[0]
    taps = 27
    weight_local = conv_weight[0].reshape(-1, taps, channels)
    steps_now = lax.dynamic_slice_in_dim(timesteps[:, 0], section_index, tick_count)
    counts_now = lax.dynamic_slice_in_dim(frame_counts[:, 0], section_index, tick_count)
    chunk_start = slab_index * chunk

    weight_cols = lax.dynamic_slice_in_dim(weight_local, chunk_start, chunk, axis=2)
    weight_chunk = gather_two_level(weight_cols, "dp", DP_INNER, low_first=False)
    kernel = weight_chunk.reshape(channels, 3, 3, 3, chunk)[:, ::-1, ::-1, ::-1, :]
    kernel = jnp.transpose(kernel, (1, 2, 3, 0, 4))


    weight_norm = 1.0 / math.sqrt(tick_count * replicas * frames * height_total * cells_wide)
    embed_norm = 1.0 / math.sqrt(frames * height_total * cells_wide)

    cot_first = jnp.where(section_index == 1, loss_cotangent[0, 0], upstream[0])
    starting = jnp.concatenate([inputs, cot_first[None], loss_cotangent[1, 0][None]])
    gathered = gather_level_into(starting, "slab", SLAB_INNER, True, 2)
    gathered = gather_level_into(gathered, "slab", SLAB_INNER, False, 2).reshape(
        2 * tick_count, frames, height_total, cells_wide, channels
    )
    inputs_chunk = lax.dynamic_slice_in_dim(gathered[:tick_count], chunk_start, chunk, axis=4)
    cot_both = gathered[tick_count:]
    cot_full_first = cot_both[0]
    cot_full_later = cot_both[1]

    dx_list = []
    embed_list = []
    hidden_list = []
    cot_list = []
    cot_full = cot_full_first
    for tick_index in range(tick_count):
        steps = steps_now[tick_index]
        count = counts_now[tick_index]
        embedded = lax.dynamic_index_in_dim(step_table, steps, keepdims=False).astype(
            jnp.float32
        )
        gain = 1.0 + lax.dynamic_slice_in_dim(embedded, chunk_start, chunk)
        bias = lax.dynamic_slice_in_dim(embedded, channels + chunk_start, chunk)
        mask = (jnp.arange(frames, dtype=jnp.int32) < count).astype(jnp.float32)
        mask_cells = mask[:, None, None, None]
        valid = count.astype(jnp.float32) * float(height_total * cells_wide * per_group)

        values = inputs_chunk[tick_index].astype(jnp.float32)
        masked = values * mask_cells
        mean_g = chunk_group_sums(masked, groups_here) / valid
        var_g = chunk_group_sums(masked * values, groups_here) / valid - mean_g * mean_g
        rstd_g = lax.rsqrt(var_g + EPS)
        mean_c = jnp.repeat(mean_g, per_group)
        rstd_c = jnp.repeat(rstd_g, per_group)
        normed = (values - mean_c) * rstd_c
        preact = normed * gain + bias
        hidden = (jax.nn.silu(preact) * mask_cells).astype(jnp.bfloat16)
        hidden_list.append(hidden)

        upward = lax.conv_general_dilated(
            cot_full[None],
            kernel,
            window_strides=(1, 1, 1),
            padding=((1, 1), (1, 1), (1, 1)),
            dimension_numbers=("NDHWC", "DHWIO", "NDHWC"),
            preferred_element_type=jnp.float32,
        )[0]
        pre_grad = upward * silu_grad(preact) * mask_cells
        dnormed = pre_grad * gain
        sum_a = chunk_group_sums(dnormed, groups_here) / valid
        sum_b = chunk_group_sums(dnormed * normed, groups_here) / valid
        scale_part = jnp.sum(pre_grad * normed, axis=(0, 1, 2))
        shift_part = jnp.sum(pre_grad, axis=(0, 1, 2))
        branch = (
            rstd_c
            * (dnormed - jnp.repeat(sum_a, per_group) - normed * jnp.repeat(sum_b, per_group))
            * mask_cells
        )
        cot_chunk = lax.dynamic_slice_in_dim(cot_full, chunk_start, chunk, axis=3)
        result = (cot_chunk.astype(jnp.float32) + branch).astype(jnp.bfloat16)
        embed_list.append(jnp.stack([scale_part, shift_part]))
        result_full = gather_level_into(result, "slab", SLAB_INNER, True, 3)
        result_full = gather_level_into(result_full, "slab", SLAB_INNER, False, 3).reshape(
            frames, height_total, cells_wide, channels
        )
        dx_list.append(
            lax.dynamic_slice_in_dim(result_full, slab_index * slab_rows, slab_rows, axis=1)
        )
        cot_list.append(cot_full)
        if tick_index + 1 < tick_count:
            received = lax.ppermute(result_full, "pipe", [(1, 0)])
            cot_full = jnp.where(section_index == 1, cot_full_later, received)

    embed_all = jnp.transpose(
        gather_two_level(jnp.stack(embed_list), "slab", SLAB_INNER), (1, 2, 0, 3)
    )
    embed_grad = embed_all.reshape(tick_count, 2 * channels) * embed_norm

    cot_all = jnp.stack(cot_list)
    hidden_all = jnp.pad(
        jnp.stack(hidden_list), ((0, 0), (1, 1), (1, 1), (1, 1), (0, 0))
    )
    hidden_taps = tap_stack(hidden_all, frames, height_total, cells_wide)
    grad_term = jnp.einsum(
        "kfrwo,tkfrwi->oti", cot_all, hidden_taps, preferred_element_type=jnp.float32
    )
    terms = (grad_term * weight_norm).astype(jnp.bfloat16)
    terms = terms.reshape(replicas, channels // replicas, taps, chunk)
    grad_shard = scatter_sum_two_level(terms, "dp", DP_INNER)
    weight_grad = gather_level_into(grad_shard.astype(jnp.bfloat16), "slab", SLAB_INNER, True, 2)
    weight_grad = gather_level_into(weight_grad, "slab", SLAB_INNER, False, 2)
    weight_grad = weight_grad.reshape(weight_grad.shape[0], taps * channels).astype(jnp.float32)
    input_grads = jnp.stack(dx_list)[None, :, None]
    return (input_grads, weight_grad[None], embed_grad[None, :, None])


def solution(mesh):
    placed = (
        P("pipe", None, "dp", None, "slab", None, None),
        P(None, "dp", None, "slab", None, None),
        P("dp", None, "slab", None, None),
        P("pipe", "dp", None),
        P("pipe", None, None),
        P(None, "dp"),
        P(None, "dp"),
    )
    return jax.shard_map(
        local,
        mesh=mesh,
        in_specs=placed,
        out_specs=(
            P("pipe", None, "dp", None, "slab", None, None),
            P("pipe", "dp", None),
            P("pipe", None, "dp", None),
        ),
        check_vma=False,
    )
```
